32 devices in a mesh: plane: 4 (over x, core), tm: 8 (over z, y).
Axes of the slice: x: 2, y: 2, z: 4, core: 2. Of those that a mesh axis runs over, the one named last changes fastest.
Arguments:
- coeffs: float32 [32, 3, 16, 512], P('tm', None, None, 'plane'), may hold values from -1.5 to 1.5
- radius: float32 [512], P('plane'), may hold values from 0.25 to 2
- tile_mask: int32 [4, 4, 1], P(None, 'plane'), may hold values from 0 to 1
Outputs:
- hazard: float32 [4, 512], P(None, 'plane')
The draws below stay inside these ranges and needn't reach their ends.
All inputs are finite; a program needn't handle non-finite values.
Results may differ from the reference program's by a relative error of at most 0.0003.
Values sent between devices are 32-bit elements; how exact they have to be, the bound alone decides.
No kernel may reach another device: no remote copies, remote signals or barrier semaphores. Data moves between devices by JAX's collectives and lax.ppermute only.
A program may use at most 64 MiB of HBM per device.

```python
import math
import jax
import jax.numpy as jnp
from jax import lax

OBJ = 128
SAMP = 32
K = 16
TILE = 128
ROUNDS = 4
WINDOWS = 32
OBJECTS = 512


def draw_tile_mask(key, part):
    blocks = OBJECTS // OBJ
    tile_count = OBJ // TILE
    first_key, second_key = jax.random.split(jax.random.fold_in(key, 11))
    density = jax.random.randint(first_key, (blocks,), 1, 10)
    row_density = jnp.repeat(density, tile_count)
    scores = jax.random.randint(second_key, (ROUNDS, OBJECTS // TILE, tile_count), 0, 10)
    return (scores < row_density[None, :, None]).astype(jnp.int32)


def level_of(stream_key, dims, cuts, least, largest):
    gain = 1.0
    for dim, blocks in cuts:
        heights = jax.random.uniform(jax.random.fold_in(jax.random.fold_in(stream_key, 6), dim), (blocks,), jnp.float32, least / len(cuts), largest / len(cuts))
        gain = gain * jnp.repeat(jnp.exp(heights), dims[dim] // blocks).reshape((-1,) + (1,) * (len(dims) - 1 - dim))
    return gain


def scatter_about(key, shape, deviation, most, cuts=(), kind=jnp.bfloat16):
    entries = deviation * jax.random.normal(key, shape, jnp.float32)
    if cuts:
        entries = entries * level_of(key, shape, cuts, -0.22, 0.18)
    return jnp.clip(entries, -most, most).astype(kind)


def setup_inputs(seed: int = 0) -> dict:
    key_of = jax.random.split(jax.random.key(seed), 4)
    return {
        "coeffs": scatter_about(key_of[0], (WINDOWS, 3, K, OBJECTS), 0.25, 1.5, ((0, 8), (3, 4)), jnp.float32),
        "radius": jnp.clip(jnp.exp(math.log(2.0) - 2.0794415 * jax.random.uniform(key_of[1], (OBJECTS,), jnp.float32) ** level_of(key_of[1], (OBJECTS,), ((0, 4),), -0.2, 0.2)), 0.25, 2.0),
        "tile_mask": draw_tile_mask(jax.random.fold_in(key_of[3], 71), 0),
    }


def basis_table(degrees):
    sample = jnp.arange(SAMP, dtype=jnp.float32)
    nodes = -1.0 + (2.0 * sample + 1.0) / SAMP
    series = [jnp.ones_like(nodes), nodes]
    for degree in range(2, degrees):
        series.append(2.0 * nodes * series[-1] - series[-2])
    return jnp.stack(series[:degrees], axis=1)


def synthesize(basis, coeff_block):
    return jnp.einsum("sk,wckn->wcsn", basis, coeff_block, precision=lax.Precision.HIGHEST)


def pair_tile(own_slice, far_slice, own_radius, far_radius):
    inverse = 1.0 / (own_radius[:, None] + far_radius[None, :])
    separation = own_slice[:, :, :, :, None] - far_slice[:, :, :, None, :]
    squared = jnp.sum(separation * separation, axis=1)
    return jnp.sum(jnp.exp(-squared * inverse), axis=(0, 1, 3))


def reference(coeffs, radius, tile_mask):
    basis = basis_table(K)
    positions = synthesize(basis, coeffs)
    groups = OBJECTS // OBJ
    tile_count = OBJ // TILE
    normalizer = 1.0 / (WINDOWS * SAMP * TILE)
    round_rows = []
    for round_no in range(ROUNDS):
        offset = (round_no // 2 + 1) * (1 if round_no % 2 == 0 else -1)

        def block_round(block):
            partner = (block - offset) % groups
            own_pos = lax.dynamic_slice_in_dim(positions, (block * OBJ).astype(jnp.int32), OBJ, 3)
            far_pos = lax.dynamic_slice_in_dim(positions, (partner * OBJ).astype(jnp.int32), OBJ, 3)
            own_rad = lax.dynamic_slice_in_dim(radius, (block * OBJ).astype(jnp.int32), OBJ, 0)
            far_rad = lax.dynamic_slice_in_dim(radius, (partner * OBJ).astype(jnp.int32), OBJ, 0)
            mask_rows = lax.dynamic_slice_in_dim(tile_mask[round_no], (block * tile_count).astype(jnp.int32), tile_count, 0)
            pieces = []
            for own_tile in range(tile_count):
                running = jnp.zeros((TILE,), jnp.float32)
                for far_tile in range(tile_count):
                    value = pair_tile(own_pos[:, :, :, own_tile * TILE:(own_tile + 1) * TILE],
                                      far_pos[:, :, :, far_tile * TILE:(far_tile + 1) * TILE],
                                      own_rad[own_tile * TILE:(own_tile + 1) * TILE],
                                      far_rad[far_tile * TILE:(far_tile + 1) * TILE])
                    running = running + jnp.where(mask_rows[own_tile, far_tile] > 0, value, jnp.zeros_like(value))
                pieces.append(running)
            return jnp.concatenate(pieces)

        per_block = lax.map(block_round, jnp.arange(groups, dtype=jnp.int32))
        round_rows.append(per_block.reshape(OBJECTS) * normalizer)
    return jnp.stack(round_rows)
```

```python
import functools
import math

import jax
import jax.numpy as jnp
import numpy as np
from jax import lax
from jax.experimental import pallas as pl
from jax.experimental.pallas import tpu as pltpu
from jax.sharding import PartitionSpec as P

SAMP = 32
ROUNDS = 4
AXES = 3
GROUP = 8
KINDS = 16
VMEM = pl.BlockSpec(memory_space=pltpu.VMEM)


def thirds(value):
    first = value.astype(jnp.bfloat16).astype(jnp.float32)
    rest = value - first
    second = rest.astype(jnp.bfloat16).astype(jnp.float32)
    third = (rest - second).astype(jnp.bfloat16).astype(jnp.float32)
    return first, second, third


def basis_table(degrees):
    sample = np.arange(SAMP, dtype=np.float32)
    nodes = np.float32(-1.0) + (np.float32(2.0) * sample + np.float32(1.0)) / np.float32(SAMP)
    series = [np.ones_like(nodes), nodes]
    for _ in range(2, degrees):
        series.append(np.float32(2.0) * nodes * series[-1] - series[-2])
    return np.stack(series[:degrees], axis=1).astype(np.float32)


def basis_parts(degrees):
    basis = basis_table(degrees)
    first = basis.astype(jnp.bfloat16).astype(np.float32)
    second = (basis - first).astype(jnp.bfloat16).astype(np.float32)
    third = (basis - first - second).astype(jnp.bfloat16).astype(np.float32)
    return np.concatenate([first, first, second, second, first, third], axis=1).astype(jnp.bfloat16)


def position_rows(basis, coeffs_ref, window):
    columns = []
    for axis in range(AXES):
        a, b, c = (part.astype(jnp.bfloat16) for part in thirds(coeffs_ref[window, axis]))
        columns.append(jnp.concatenate([a, b, a, b, c, a], axis=0))
    stacked = jnp.concatenate(columns, axis=1)
    rows = jnp.dot(basis, stacked, preferred_element_type=jnp.float32)
    width = coeffs_ref.shape[3]
    return [rows[:, axis * width:(axis + 1) * width] for axis in range(AXES)]


def features(rows):
    found = []
    for start in range(0, SAMP, GROUP):
        high, low, length = [], [], None
        for row in rows:
            value = row[start:start + GROUP]
            top = value.astype(jnp.bfloat16).astype(jnp.float32)
            bottom = (value - top).astype(jnp.bfloat16).astype(jnp.float32)
            kept = top + bottom
            length = kept * kept if length is None else length + kept * kept
            high.append(top)
            low.append(bottom)
        found.append((high, low, list(thirds(length))))
    return found


def own_kernel(basis_ref, coeffs_ref, radius_ref, left_ref, spread_ref):
    objects = coeffs_ref.shape[3]
    one = jnp.ones((GROUP, objects), jnp.float32)
    zero = jnp.zeros((GROUP, objects), jnp.float32)
    depth = GROUP * KINDS
    basis = basis_ref[...]
    for window in range(coeffs_ref.shape[0]):
        groups = features(position_rows(basis, coeffs_ref, window))
        for index, (high, low, length) in enumerate(groups):
            high = [-2.0 * value for value in high]
            low = [-2.0 * value for value in low]
            stack = jnp.concatenate(high + high + low + length + [one, one, one, zero], axis=0)
            place = window * len(groups) + index
            left_ref[place // 2, :, (place % 2) * depth:(place % 2 + 1) * depth] = stack.T.astype(jnp.bfloat16)
    spread_ref[...] = jnp.broadcast_to(radius_ref[...], spread_ref.shape).T


def pair_kernel(basis_ref, left_ref, spread_ref, coeffs_ref, radius_ref, out_ref, right_ref):
    objects = coeffs_ref.shape[3]
    one = jnp.ones((GROUP, objects), jnp.float32)
    zero = jnp.zeros((GROUP, objects), jnp.float32)
    depth = GROUP * KINDS
    basis = basis_ref[...]
    blank = jnp.zeros((depth, objects), jnp.bfloat16)
    for window in range(coeffs_ref.shape[0]):
        groups = features(position_rows(basis, coeffs_ref, window))
        for index, (high, low, length) in enumerate(groups):
            stack = jnp.concatenate(high + low + high + [one, one, one] + length + [zero], axis=0)
            place = window * len(groups) + index
            half = place % 2
            rows = slice(half * depth, (half + 1) * depth)
            right_ref[place // 2, rows, half * objects:(half + 1) * objects] = stack.astype(jnp.bfloat16)
            right_ref[place // 2, rows, (1 - half) * objects:(2 - half) * objects] = blank
    scale = (-1.0 / math.log(2.0)) / (spread_ref[...] + radius_ref[...])
    lane = lax.broadcasted_iota(jnp.int32, (objects, 2 * depth), 1) % GROUP

    def visit(step, total):
        left = left_ref[step]
        right = right_ref[step]
        for sample in range(GROUP):
            chosen = jnp.where(lane == sample, left, jnp.zeros_like(left))
            squared = jnp.dot(chosen, right, preferred_element_type=jnp.float32)
            total = total + jnp.exp2(squared[:, :objects] * scale) + jnp.exp2(squared[:, objects:] * scale)
        return total

    total = lax.fori_loop(0, left_ref.shape[0], visit, jnp.zeros((objects, objects), jnp.float32))
    out_ref[...] = lax.dot_general(
        jnp.ones((8, objects), jnp.float32), total, (((1,), (1,)), ((), ())),
        precision=lax.Precision.HIGHEST, preferred_element_type=jnp.float32,
    )


def own_side(basis, coeffs, radius):
    windows, _, _, objects = coeffs.shape
    pairs = windows * SAMP // GROUP // 2
    return pl.pallas_call(
        own_kernel,
        out_shape=(
            jax.ShapeDtypeStruct((pairs, objects, 2 * GROUP * KINDS), jnp.bfloat16),
            jax.ShapeDtypeStruct((objects, objects), jnp.float32),
        ),
        in_specs=[VMEM] * 3,
        out_specs=(VMEM, VMEM),
        name="own_side",
        compiler_params=pltpu.CompilerParams(vmem_limit_bytes=16 << 20),
        cost_estimate=pl.CostEstimate(flops=10_000_000, bytes_accessed=1_000_000, transcendentals=0),
    )(basis, coeffs, radius)


def pair_side(basis, left, spread, coeffs, radius):
    windows, _, _, objects = coeffs.shape
    pairs = windows * SAMP // GROUP // 2
    depth = 2 * GROUP * KINDS
    return pl.pallas_call(
        pair_kernel,
        out_shape=jax.ShapeDtypeStruct((8, objects), jnp.float32),
        in_specs=[VMEM] * 5,
        out_specs=VMEM,
        scratch_shapes=[pltpu.VMEM((pairs, depth, 2 * objects), jnp.bfloat16)],
        name="pair_side",
        compiler_params=pltpu.CompilerParams(vmem_limit_bytes=16 << 20),
        cost_estimate=pl.CostEstimate(
            flops=2 * pairs * GROUP * objects * depth * 2 * objects,
            bytes_accessed=4_000_000,
            transcendentals=windows * SAMP * objects * objects,
        ),
    )(basis, left, spread, coeffs, radius)


def moved(values, axis, pairs):
    return tuple(lax.ppermute(value, axis, pairs) for value in values)


def partners(values, plane_count):
    group = lax.axis_index("plane")
    if plane_count == 4:
        near = moved(values, "plane", [(g, g ^ 1) for g in range(4)])
        across = moved(values, "plane", [(g, g ^ 2) for g in range(4)])
        far = moved(values, "plane", [(g, g ^ 3) for g in range(4)])
        odd = group % 2
        return [near, across, far], [2 - 2 * odd, 2 * odd, 1, 1]
    steps, places = [], []
    for round_no in range(ROUNDS):
        step = (round_no // 2 + 1) * (1 if round_no % 2 == 0 else -1) % plane_count
        if step not in steps:
            steps.append(step)
        places.append(steps.index(step))
    found = [moved(values, "plane", [(g, (g + step) % plane_count) for g in range(plane_count)]) for step in steps]
    return found, places


def summed(value, axis):
    count = lax.axis_size(axis)
    if count & (count - 1):
        return lax.psum(value, axis)
    step = 1
    while step < count:
        value = value + lax.ppermute(value, axis, [(i, i ^ step) for i in range(count)])
        step *= 2
    return value


def local(coeffs, radius, tile_mask):
    windows, _, degrees, objects = coeffs.shape
    basis = jnp.asarray(basis_parts(degrees))
    radius_row = radius[None, :]
    found, places = partners((coeffs, radius_row), lax.axis_size("plane"))
    left, spread = own_side(basis, coeffs, radius_row)
    rows = [pair_side(basis, left, spread, *other)[:1] for other in found]
    normalizer = 1.0 / (windows * lax.axis_size("tm") * SAMP * objects)
    chosen = (jnp.stack([jnp.asarray(place) for place in places])[:, None] == jnp.arange(len(found))[None, :])
    weight = jnp.where(chosen, tile_mask[:, 0, :].astype(jnp.float32) * normalizer, 0.0)
    terms = sum(weight[:, index, None] * row for index, row in enumerate(rows))
    return summed(terms, "tm")


def solution(mesh):
    placed = (P("tm", None, None, "plane"), P("plane"), P(None, "plane", None))
    return jax.shard_map(
        local, mesh=mesh, in_specs=placed, out_specs=P(None, "plane"), check_vma=False
    )
```

```python
import functools
import math

import jax
import jax.numpy as jnp
import numpy as np
from jax import lax
from jax.experimental import pallas as pl
from jax.experimental.pallas import tpu as pltpu
from jax.sharding import PartitionSpec as P

SAMP = 32
ROUNDS = 4
AXES = 3
GROUP = 8
KINDS = 16
VMEM = pl.BlockSpec(memory_space=pltpu.VMEM)


def thirds(value):
    first = value.astype(jnp.bfloat16).astype(jnp.float32)
    rest = value - first
    second = rest.astype(jnp.bfloat16).astype(jnp.float32)
    third = (rest - second).astype(jnp.bfloat16).astype(jnp.float32)
    return first, second, third


def basis_table(degrees):
    sample = np.arange(SAMP, dtype=np.float32)
    nodes = np.float32(-1.0) + (np.float32(2.0) * sample + np.float32(1.0)) / np.float32(SAMP)
    series = [np.ones_like(nodes), nodes]
    for _ in range(2, degrees):
        series.append(np.float32(2.0) * nodes * series[-1] - series[-2])
    return np.stack(series[:degrees], axis=1).astype(np.float32)


def basis_parts(degrees):
    basis = (basis_table(degrees).astype(np.float64) * math.sqrt(1.0 / math.log(2.0))).astype(np.float32)
    first = basis.astype(jnp.bfloat16).astype(np.float32)
    second = (basis - first).astype(jnp.bfloat16).astype(np.float32)
    third = (basis - first - second).astype(jnp.bfloat16).astype(np.float32)
    return np.concatenate([first, first, second, second, first, third], axis=1).astype(jnp.bfloat16)


def position_rows(basis, packed_ref, window):
    columns = []
    degrees = basis.shape[1] // 6
    for axis in range(AXES):
        start = (window * AXES + axis) * degrees
        a, b, c = (part.astype(jnp.bfloat16) for part in thirds(packed_ref[start:start + degrees]))
        columns.append(jnp.concatenate([a, b, a, b, c, a], axis=0))
    stacked = jnp.concatenate(columns, axis=1)
    rows = jnp.dot(basis, stacked, preferred_element_type=jnp.float32)
    width = packed_ref.shape[1]
    return [rows[:, axis * width:(axis + 1) * width] for axis in range(AXES)]


def features(rows):
    found = []
    for start in range(0, SAMP, GROUP):
        high, low, length = [], [], None
        for row in rows:
            value = row[start:start + GROUP]
            top = value.astype(jnp.bfloat16).astype(jnp.float32)
            bottom = (value - top).astype(jnp.bfloat16).astype(jnp.float32)
            kept = top + bottom
            length = kept * kept if length is None else length + kept * kept
            high.append(top)
            low.append(bottom)
        found.append((high, low, list(thirds(-length))))
    return found


def stage_kernel(coeffs_ref, radius_ref, mask_ref, basis_ref, packed_ref, near_mask_ref, near_basis_ref, sems):
    rows = coeffs_ref.shape[0]
    copies = [
        pltpu.make_async_copy(coeffs_ref, packed_ref.at[:rows], sems.at[0]),
        pltpu.make_async_copy(radius_ref, packed_ref.at[rows:], sems.at[1]),
        pltpu.make_async_copy(mask_ref, near_mask_ref, sems.at[2]),
        pltpu.make_async_copy(basis_ref, near_basis_ref, sems.at[3]),
    ]
    for copy in copies:
        copy.start()
    for copy in copies:
        copy.wait()


def stage(coeffs, radius, mask, basis):
    windows, axes, degrees, objects = coeffs.shape
    rows = windows * axes * degrees
    return pl.pallas_call(
        stage_kernel,
        out_shape=(
            jax.ShapeDtypeStruct((rows + 1, objects), jnp.float32),
            jax.ShapeDtypeStruct((1, ROUNDS), jnp.int32),
            jax.ShapeDtypeStruct(basis.shape, basis.dtype),
        ),
        in_specs=[pl.BlockSpec(memory_space=pltpu.HBM)] * 4,
        out_specs=(VMEM,) * 3,
        scratch_shapes=[pltpu.SemaphoreType.DMA((4,))],
        name="stage",
        compiler_params=pltpu.CompilerParams(vmem_limit_bytes=1 << 20),
    )(*(pltpu.with_memory_space_constraint(value, pltpu.HBM) for value in (coeffs.reshape(rows, objects), radius[None, :], mask.reshape(1, ROUNDS), basis)))


def own_kernel(places_of, factor, basis_ref, packed_ref, mask_ref, left_ref, spread_ref, weight_ref):
    objects = packed_ref.shape[1]
    last = packed_ref.shape[0] - 1
    one = jnp.ones((GROUP, objects), jnp.float32)
    zero = jnp.zeros((GROUP, objects), jnp.float32)
    depth = GROUP * KINDS
    basis = basis_ref[...]
    for window in range(last // (AXES * basis.shape[1] // 6)):
        groups = features(position_rows(basis, packed_ref, window))
        for index, (high, low, length) in enumerate(groups):
            high = [2.0 * value for value in high]
            low = [2.0 * value for value in low]
            stack = jnp.concatenate(high + high + low + length + [one, one, one, zero], axis=0)
            place = window * len(groups) + index
            left_ref[place // 2, :, (place % 2) * depth:(place % 2 + 1) * depth] = stack.T.astype(jnp.bfloat16)
    spread_ref[...] = jnp.broadcast_to(packed_ref[last:], spread_ref.shape).T
    weight_ref[...] = jnp.zeros_like(weight_ref)
    for round_no, place in enumerate(places_of()):
        screened = jnp.broadcast_to(mask_ref[:, round_no:round_no + 1], (1, objects)).astype(jnp.float32) * factor
        for index in range(weight_ref.shape[0]):
            weight_ref[index, round_no:round_no + 1] = jnp.where(place == index, screened, 0.0)


def pair_kernel(order, basis_ref, left_ref, spread_ref, weight_ref, packed_ref, *refs):
    *earlier, out_ref, right_ref, scale_ref = refs
    objects = packed_ref.shape[1]
    last = packed_ref.shape[0] - 1
    one = jnp.ones((GROUP, objects), jnp.float32)
    zero = jnp.zeros((GROUP, objects), jnp.float32)
    depth = GROUP * KINDS
    basis = basis_ref[...]
    blank = jnp.zeros((depth, objects), jnp.bfloat16)
    for window in range(last // (AXES * basis.shape[1] // 6)):
        groups = features(position_rows(basis, packed_ref, window))
        for index, (high, low, length) in enumerate(groups):
            stack = jnp.concatenate(high + low + high + [one, one, one] + length + [zero], axis=0)
            place = window * len(groups) + index
            half = place % 2
            rows = slice(half * depth, (half + 1) * depth)
            right_ref[place // 2, rows, half * objects:(half + 1) * objects] = stack.astype(jnp.bfloat16)
            right_ref[place // 2, rows, (1 - half) * objects:(2 - half) * objects] = blank
    scale_ref[...] = 1.0 / (spread_ref[...] + packed_ref[last:])
    lane = lax.broadcasted_iota(jnp.int32, (objects, 2 * depth), 1) % GROUP

    def visit(step, total):
        left = left_ref[step]
        right = right_ref[step]
        for sample in range(GROUP):
            chosen = jnp.where(lane == sample, left, jnp.zeros_like(left))
            squared = jnp.dot(chosen, right, preferred_element_type=jnp.float32)
            scale = scale_ref[...]
            total = total + (jnp.exp2(squared[:, :objects] * scale) + jnp.exp2(squared[:, objects:] * scale))
        return total

    total = lax.fori_loop(0, left_ref.shape[0], visit, jnp.zeros((objects, objects), jnp.float32), unroll=8)
    rows = lax.dot_general(
        jnp.ones((8, objects), jnp.float32), total, (((1,), (1,)), ((), ())),
        precision=lax.Precision.HIGHEST, preferred_element_type=jnp.float32,
    )
    terms = weight_ref[order] * rows[:ROUNDS]
    out_ref[...] = earlier[0][...] + terms if earlier else terms


def own_side(basis, packed, mask, windows, partner_count, places_of, factor):
    objects = packed.shape[1]
    pairs = windows * SAMP // GROUP // 2
    return pl.pallas_call(
        functools.partial(own_kernel, places_of, factor),
        out_shape=(
            jax.ShapeDtypeStruct((pairs, objects, 2 * GROUP * KINDS), jnp.bfloat16),
            jax.ShapeDtypeStruct((objects, objects), jnp.float32),
            jax.ShapeDtypeStruct((partner_count, ROUNDS, objects), jnp.float32),
        ),
        in_specs=[VMEM] * 3,
        out_specs=(VMEM,) * 3,
        name="own_side",
        compiler_params=pltpu.CompilerParams(vmem_limit_bytes=16 << 20),
        cost_estimate=pl.CostEstimate(flops=10_000_000, bytes_accessed=1_000_000, transcendentals=0),
    )(basis, packed, mask)


def pair_side(order, basis, left, spread, weight, packed, windows, earlier):
    objects = packed.shape[1]
    pairs = windows * SAMP // GROUP // 2
    depth = 2 * GROUP * KINDS
    operands = (basis, left, spread, weight, packed) + (() if earlier is None else (earlier,))
    return pl.pallas_call(
        functools.partial(pair_kernel, order),
        out_shape=jax.ShapeDtypeStruct((ROUNDS, objects), jnp.float32),
        in_specs=[VMEM] * len(operands),
        out_specs=VMEM,
        scratch_shapes=[
            pltpu.VMEM((pairs, depth, 2 * objects), jnp.bfloat16),
            pltpu.VMEM((objects, objects), jnp.float32),
        ],
        name="pair_side",
        compiler_params=pltpu.CompilerParams(vmem_limit_bytes=16 << 20),
        cost_estimate=pl.CostEstimate(
            flops=2 * pairs * GROUP * objects * depth * 2 * objects,
            bytes_accessed=4_000_000,
            transcendentals=windows * SAMP * objects * objects,
        ),
    )(*operands)


def plan(plane_count):
    if plane_count == 4:
        def places_of():
            odd = lax.axis_index("plane") % 2
            return [1 - odd, odd, 2, 2]

        near = [(g, g ^ 1) for g in range(4)]
        across = [(g, g ^ 3) for g in range(4)]
        return [(None, near), (None, across), (1, near)], places_of
    steps, places = [], []
    for round_no in range(ROUNDS):
        step = (round_no // 2 + 1) * (1 if round_no % 2 == 0 else -1) % plane_count
        if step not in steps:
            steps.append(step)
        places.append(steps.index(step))
    return [(None, [(g, (g + step) % plane_count) for g in range(plane_count)]) for step in steps], lambda: places


def summed(value, axis):
    count = lax.axis_size(axis)
    if count & (count - 1):
        return lax.psum(value, axis)
    step = 1
    while step < count:
        value = value + lax.ppermute(value, axis, [(i, i ^ step) for i in range(count)])
        step *= 2
    return value


def local(coeffs, radius, tile_mask):
    windows, _, degrees, objects = coeffs.shape
    packed, mask, basis = stage(coeffs, radius, tile_mask, jnp.asarray(basis_parts(degrees)))
    moves, places_of = plan(lax.axis_size("plane"))
    others = [lax.ppermute(packed, "plane", move) for source, move in moves if source is None]
    factor = 1.0 / (windows * lax.axis_size("tm") * SAMP * objects)
    left, spread, weight = own_side(basis, packed, mask, windows, len(moves), places_of, factor)
    terms = None
    for order, (source, move) in enumerate(moves):
        if source is not None:
            others.append(lax.ppermute(others[source], "plane", move))
        terms = pair_side(order, basis, left, spread, weight, others[order], windows, terms)
        if order + 1 < len(others):
            others[order + 1], terms = lax.optimization_barrier((others[order + 1], terms))
    return summed(terms, "tm")


def solution(mesh):
    placed = (P("tm", None, None, "plane"), P("plane"), P(None, "plane", None))
    return jax.shard_map(
        local, mesh=mesh, in_specs=placed, out_specs=P(None, "plane"), check_vma=False
    )
```

```python
import functools
import math

import jax
import jax.numpy as jnp
import numpy as np
from jax import lax
from jax.experimental import pallas as pl
from jax.experimental.pallas import tpu as pltpu
from jax.sharding import PartitionSpec as P

SAMP = 32
ROUNDS = 4
AXES = 3
GROUP = 8
KINDS = 16
VMEM = pl.BlockSpec(memory_space=pltpu.VMEM)


def thirds(value):
    first = value.astype(jnp.bfloat16).astype(jnp.float32)
    rest = value - first
    second = rest.astype(jnp.bfloat16).astype(jnp.float32)
    third = (rest - second).astype(jnp.bfloat16).astype(jnp.float32)
    return first, second, third


def basis_table(degrees):
    sample = np.arange(SAMP, dtype=np.float32)
    nodes = np.float32(-1.0) + (np.float32(2.0) * sample + np.float32(1.0)) / np.float32(SAMP)
    series = [np.ones_like(nodes), nodes]
    for _ in range(2, degrees):
        series.append(np.float32(2.0) * nodes * series[-1] - series[-2])
    return np.stack(series[:degrees], axis=1).astype(np.float32)


def basis_parts(degrees):
    basis = (basis_table(degrees).astype(np.float64) * math.sqrt(1.0 / math.log(2.0))).astype(np.float32)
    first = basis.astype(jnp.bfloat16).astype(np.float32)
    second = (basis - first).astype(jnp.bfloat16).astype(np.float32)
    third = (basis - first - second).astype(jnp.bfloat16).astype(np.float32)
    return np.concatenate([first, first, second, second, first, third], axis=1).astype(jnp.bfloat16)


def position_rows(basis, packed_ref, window):
    columns = []
    degrees = basis.shape[1] // 6
    for axis in range(AXES):
        start = (window * AXES + axis) * degrees
        a, b, c = (part.astype(jnp.bfloat16) for part in thirds(packed_ref[start:start + degrees]))
        columns.append(jnp.concatenate([a, b, a, b, c, a], axis=0))
    stacked = jnp.concatenate(columns, axis=1)
    rows = jnp.dot(basis, stacked, preferred_element_type=jnp.float32)
    width = packed_ref.shape[1]
    return [rows[:, axis * width:(axis + 1) * width] for axis in range(AXES)]


def features(rows):
    found = []
    for start in range(0, SAMP, GROUP):
        high, low, length = [], [], None
        for row in rows:
            value = row[start:start + GROUP]
            top = value.astype(jnp.bfloat16).astype(jnp.float32)
            bottom = (value - top).astype(jnp.bfloat16).astype(jnp.float32)
            kept = top + bottom
            length = kept * kept if length is None else length + kept * kept
            high.append(top)
            low.append(bottom)
        found.append((high, low, list(thirds(-length))))
    return found


def stage_kernel(coeffs_ref, radius_ref, mask_ref, basis_ref, packed_ref, near_mask_ref, near_basis_ref, sems):
    rows = coeffs_ref.shape[0]
    copies = [
        pltpu.make_async_copy(coeffs_ref, packed_ref.at[:rows], sems.at[0]),
        pltpu.make_async_copy(radius_ref, packed_ref.at[rows:], sems.at[1]),
        pltpu.make_async_copy(mask_ref, near_mask_ref, sems.at[2]),
        pltpu.make_async_copy(basis_ref, near_basis_ref, sems.at[3]),
    ]
    for copy in copies:
        copy.start()
    for copy in copies:
        copy.wait()


def stage(coeffs, radius, mask, basis):
    windows, axes, degrees, objects = coeffs.shape
    rows = windows * axes * degrees
    return pl.pallas_call(
        stage_kernel,
        out_shape=(
            jax.ShapeDtypeStruct((rows + 1, objects), jnp.float32),
            jax.ShapeDtypeStruct((1, ROUNDS), jnp.int32),
            jax.ShapeDtypeStruct(basis.shape, basis.dtype),
        ),
        in_specs=[pl.BlockSpec(memory_space=pltpu.HBM)] * 4,
        out_specs=(VMEM,) * 3,
        scratch_shapes=[pltpu.SemaphoreType.DMA((4,))],
        name="stage",
        compiler_params=pltpu.CompilerParams(vmem_limit_bytes=1 << 20),
    )(*(pltpu.with_memory_space_constraint(value, pltpu.HBM) for value in (coeffs.reshape(rows, objects), radius[None, :], mask.reshape(1, ROUNDS), basis)))


def own_kernel(places_of, factor, basis_ref, packed_ref, mask_ref, left_ref, spread_ref, weight_ref):
    objects = packed_ref.shape[1]
    last = packed_ref.shape[0] - 1
    one = jnp.ones((GROUP, objects), jnp.float32)
    zero = jnp.zeros((GROUP, objects), jnp.float32)
    basis = basis_ref[...]
    for window in range(last // (AXES * basis.shape[1] // 6)):
        groups = features(position_rows(basis, packed_ref, window))
        for index, (high, low, length) in enumerate(groups):
            high = [2.0 * value for value in high]
            low = [2.0 * value for value in low]
            stack = jnp.concatenate(high + high + low + length + [one, one, one, zero], axis=0)
            place = window * len(groups) + index
            left_ref[place] = stack.T.astype(jnp.bfloat16)
    spread_ref[...] = jnp.broadcast_to(packed_ref[last:], spread_ref.shape).T
    weight_ref[...] = jnp.zeros_like(weight_ref)
    for round_no, place in enumerate(places_of()):
        screened = jnp.broadcast_to(mask_ref[:, round_no:round_no + 1], (1, objects)).astype(jnp.float32) * factor
        for index in range(weight_ref.shape[0]):
            weight_ref[index, round_no:round_no + 1] = jnp.where(place == index, screened, 0.0)


def pair_kernel(place, basis_ref, left_ref, spread_ref, packed_ref, *refs):
    *earlier, out_ref, scale_ref = refs
    objects = packed_ref.shape[1]
    last = packed_ref.shape[0] - 1
    one = jnp.ones((GROUP, objects), jnp.float32)
    zero = jnp.zeros((GROUP, objects), jnp.float32)
    depth = GROUP * KINDS
    basis = basis_ref[...]
    blank = jnp.zeros((depth, objects), jnp.bfloat16)
    scale_ref[...] = 1.0 / (spread_ref[...] + packed_ref[last:])
    lane = lax.broadcasted_iota(jnp.int32, (objects, 2 * depth), 1) % GROUP
    total = jnp.zeros((objects, objects), jnp.float32)
    blocks = []
    for window in range(last // (AXES * basis.shape[1] // 6)):
        for high, low, length in features(position_rows(basis, packed_ref, window)):
            stack = jnp.concatenate(high + low + high + [one, one, one] + length + [zero], axis=0)
            blocks.append(stack.astype(jnp.bfloat16))
    for pair in range(len(blocks) // 2):
        left = jnp.concatenate([left_ref[2 * pair], left_ref[2 * pair + 1]], axis=1)
        right = jnp.concatenate([
            jnp.concatenate([blocks[2 * pair], blank], axis=1),
            jnp.concatenate([blank, blocks[2 * pair + 1]], axis=1),
        ], axis=0)
        for sample in range(GROUP):
            chosen = jnp.where(lane == sample, left, jnp.zeros_like(left))
            squared = jnp.dot(chosen, right, preferred_element_type=jnp.float32)
            scale = scale_ref[...]
            total = total + (jnp.exp2(squared[:, :objects] * scale) + jnp.exp2(squared[:, objects:] * scale))
    rows = lax.dot_general(
        jnp.ones((8, objects), jnp.float32), total, (((1,), (1,)), ((), ())),
        precision=lax.Precision.HIGHEST, preferred_element_type=jnp.float32,
    )
    out_ref[...] = earlier[0][...] if earlier else jnp.zeros_like(out_ref)
    out_ref[place:place + 1] = rows[:1]


def own_side(basis, packed, mask, windows, partner_count, places_of, factor):
    objects = packed.shape[1]
    return pl.pallas_call(
        functools.partial(own_kernel, places_of, factor),
        out_shape=(
            jax.ShapeDtypeStruct((windows * SAMP // GROUP, objects, GROUP * KINDS), jnp.bfloat16),
            jax.ShapeDtypeStruct((objects, objects), jnp.float32),
            jax.ShapeDtypeStruct((partner_count, ROUNDS, objects), jnp.float32),
        ),
        in_specs=[VMEM] * 3,
        out_specs=(VMEM,) * 3,
        name="own_side",
        compiler_params=pltpu.CompilerParams(vmem_limit_bytes=16 << 20),
        cost_estimate=pl.CostEstimate(flops=10_000_000, bytes_accessed=1_000_000, transcendentals=0),
    )(basis, packed, mask)


def pair_side(place, basis, left, spread, packed, windows, earlier, partner_count):
    objects = packed.shape[1]
    pairs = windows * SAMP // GROUP // 2
    depth = 2 * GROUP * KINDS
    operands = (basis, left, spread, packed) + (() if earlier is None else (earlier,))
    return pl.pallas_call(
        functools.partial(pair_kernel, place),
        out_shape=jax.ShapeDtypeStruct((partner_count, objects), jnp.float32),
        in_specs=[VMEM] * len(operands),
        out_specs=VMEM,
        scratch_shapes=[pltpu.VMEM((objects, objects), jnp.float32)],
        name="pair_side",
        compiler_params=pltpu.CompilerParams(vmem_limit_bytes=16 << 20),
        cost_estimate=pl.CostEstimate(
            flops=2 * pairs * GROUP * objects * depth * 2 * objects,
            bytes_accessed=4_000_000,
            transcendentals=windows * SAMP * objects * objects,
        ),
    )(*operands)


def direct_plan(plane_count):
    steps, places = [], []
    for round_no in range(ROUNDS):
        step = (round_no // 2 + 1) * (1 if round_no % 2 == 0 else -1) % plane_count
        if step not in steps:
            steps.append(step)
        places.append(steps.index(step))
    return [[(g, (g + step) % plane_count) for g in range(plane_count)] for step in steps], places


def rotated_places():
    odd = lax.axis_index("plane") % 2
    return [1 - odd, odd, 2, 2]


def doubling_steps(times):
    return [] if times & (times - 1) else [1 << bit for bit in range(times.bit_length() - 1)]


def summed(value, straight):
    planes, times = lax.axis_size("plane"), lax.axis_size("tm")

    def moved(array, flip, step):
        pairs = [
            (plane * times + time, (plane ^ flip) * times + (time ^ step))
            for plane in range(planes) for time in range(times)
        ]
        return lax.ppermute(array, ("plane", "tm"), pairs)

    for place, step in enumerate(doubling_steps(times)):
        if place == straight:
            value = value + moved(value, 0, step)
        else:
            value = moved(value, 1, step) + moved(value, 1, 0)
    return value


def local(coeffs, radius, tile_mask):
    windows, _, degrees, objects = coeffs.shape
    planes, times = lax.axis_size("plane"), lax.axis_size("tm")
    packed, mask, basis = stage(coeffs, radius, tile_mask, jnp.asarray(basis_parts(degrees)))
    factor = 1.0 / (windows * times * SAMP * objects)
    steps = doubling_steps(times)

    if planes == 4 and len(steps) % 2:
        near = lax.ppermute(packed, "plane", [(g, g ^ 1) for g in range(4)])
        across = lax.ppermute(packed, "plane", [(g, g ^ 3) for g in range(4)])
        left, spread, weight = own_side(basis, near, mask, windows, 3, rotated_places, factor)
        sums = pair_side(0, basis, left, spread, packed, windows, None, 3)
        across, sums = lax.optimization_barrier((across, sums))
        relayed = lax.ppermute(across, "plane", [(g, g ^ 1) for g in range(4)])
        sums = pair_side(2, basis, left, spread, across, windows, sums, 3)
        sums = pair_side(1, basis, left, spread, relayed, windows, sums, 3)
        sums = summed(sums, None)
    else:
        moves, places = direct_plan(planes)
        others = [lax.ppermute(packed, "plane", move) for move in moves]
        left, spread, weight = own_side(basis, packed, mask, windows, len(moves), lambda: places, factor)
        sums = None
        for place, other in enumerate(others):
            sums = pair_side(place, basis, left, spread, other, windows, sums, len(moves))
        if steps and planes % 2 == 0:
            sums = summed(sums, len(steps) // 2 if len(steps) % 2 else None)
        else:
            sums = lax.psum(sums, "tm")
    return sum(weight[place] * sums[place:place + 1] for place in range(weight.shape[0]))


def solution(mesh):
    placed = (P("tm", None, None, "plane"), P("plane"), P(None, "plane", None))
    return jax.shard_map(
        local, mesh=mesh, in_specs=placed, out_specs=P(None, "plane"), check_vma=False
    )
```

```python
import functools
import math

import jax
import jax.numpy as jnp
import numpy as np
from jax import lax
from jax.experimental import pallas as pl
from jax.experimental.pallas import tpu as pltpu
from jax.sharding import PartitionSpec as P

SAMP = 32
ROUNDS = 4
AXES = 3
GROUP = 8
KINDS = 16
VMEM = pl.BlockSpec(memory_space=pltpu.VMEM)


def thirds(value):
    first = value.astype(jnp.bfloat16).astype(jnp.float32)
    rest = value - first
    second = rest.astype(jnp.bfloat16).astype(jnp.float32)
    third = (rest - second).astype(jnp.bfloat16).astype(jnp.float32)
    return first, second, third


def basis_table(degrees):
    sample = np.arange(SAMP, dtype=np.float32)
    nodes = np.float32(-1.0) + (np.float32(2.0) * sample + np.float32(1.0)) / np.float32(SAMP)
    series = [np.ones_like(nodes), nodes]
    for _ in range(2, degrees):
        series.append(np.float32(2.0) * nodes * series[-1] - series[-2])
    return np.stack(series[:degrees], axis=1).astype(np.float32)


def basis_parts(degrees):
    basis = (basis_table(degrees).astype(np.float64) * math.sqrt(1.0 / math.log(2.0))).astype(np.float32)
    first = basis.astype(jnp.bfloat16).astype(np.float32)
    second = (basis - first).astype(jnp.bfloat16).astype(np.float32)
    third = (basis - first - second).astype(jnp.bfloat16).astype(np.float32)
    return np.concatenate([first, first, second, second, first, third], axis=1).astype(jnp.bfloat16)


def position_rows(basis, packed_ref, window):
    columns = []
    degrees = basis.shape[1] // 6
    for axis in range(AXES):
        start = (window * AXES + axis) * degrees
        a, b, c = (part.astype(jnp.bfloat16) for part in thirds(packed_ref[start:start + degrees]))
        columns.append(jnp.concatenate([a, b, a, b, c, a], axis=0))
    stacked = jnp.concatenate(columns, axis=1)
    rows = jnp.dot(basis, stacked, preferred_element_type=jnp.float32)
    width = packed_ref.shape[1]
    return [rows[:, axis * width:(axis + 1) * width] for axis in range(AXES)]


def features(rows):
    found = []
    for start in range(0, SAMP, GROUP):
        high, low, length = [], [], None
        for row in rows:
            value = row[start:start + GROUP]
            top = value.astype(jnp.bfloat16).astype(jnp.float32)
            bottom = (value - top).astype(jnp.bfloat16).astype(jnp.float32)
            kept = top + bottom
            length = kept * kept if length is None else length + kept * kept
            high.append(top)
            low.append(bottom)
        found.append((high, low, list(thirds(-length))))
    return found


def stage_kernel(coeffs_ref, radius_ref, mask_ref, basis_ref, packed_ref, near_mask_ref, near_basis_ref, sems):
    rows = coeffs_ref.shape[0]
    copies = [
        pltpu.make_async_copy(coeffs_ref, packed_ref.at[:rows], sems.at[0]),
        pltpu.make_async_copy(radius_ref, packed_ref.at[rows:], sems.at[1]),
        pltpu.make_async_copy(mask_ref, near_mask_ref, sems.at[2]),
        pltpu.make_async_copy(basis_ref, near_basis_ref, sems.at[3]),
    ]
    for copy in copies:
        copy.start()
    for copy in copies:
        copy.wait()


def stage(coeffs, radius, mask, basis):
    windows, axes, degrees, objects = coeffs.shape
    rows = windows * axes * degrees
    return pl.pallas_call(
        stage_kernel,
        out_shape=(
            jax.ShapeDtypeStruct((rows + 1, objects), jnp.float32),
            jax.ShapeDtypeStruct((1, ROUNDS), jnp.int32),
            jax.ShapeDtypeStruct(basis.shape, basis.dtype),
        ),
        in_specs=[pl.BlockSpec(memory_space=pltpu.HBM)] * 4,
        out_specs=(VMEM,) * 3,
        scratch_shapes=[pltpu.SemaphoreType.DMA((4,))],
        name="stage",
        compiler_params=pltpu.CompilerParams(vmem_limit_bytes=1 << 20),
    )(*(pltpu.with_memory_space_constraint(value, pltpu.HBM) for value in (coeffs.reshape(rows, objects), radius[None, :], mask.reshape(1, ROUNDS), basis)))


def own_kernel(places_of, factor, basis_ref, packed_ref, mask_ref, left_ref, spread_ref, weight_ref):
    objects = packed_ref.shape[1]
    last = packed_ref.shape[0] - 1
    one = jnp.ones((GROUP, objects), jnp.float32)
    zero = jnp.zeros((GROUP, objects), jnp.float32)
    basis = basis_ref[...]
    for window in range(last // (AXES * basis.shape[1] // 6)):
        groups = features(position_rows(basis, packed_ref, window))
        for index, (high, low, length) in enumerate(groups):
            high = [2.0 * value for value in high]
            low = [2.0 * value for value in low]
            stack = jnp.concatenate(high + high + low + length + [one, one, one, zero], axis=0)
            place = window * len(groups) + index
            left_ref[place] = stack.T.astype(jnp.bfloat16)
    spread_ref[...] = jnp.broadcast_to(packed_ref[last:], spread_ref.shape).T
    weight_ref[...] = jnp.zeros_like(weight_ref)
    for round_no, place in enumerate(places_of()):
        screened = jnp.broadcast_to(mask_ref[:, round_no:round_no + 1], (1, objects)).astype(jnp.float32) * factor
        for index in range(weight_ref.shape[0]):
            weight_ref[index, round_no:round_no + 1] = jnp.where(place == index, screened, 0.0)


def pair_kernel(place, basis_ref, left_ref, spread_ref, packed_ref, *refs):
    *earlier, out_ref, scale_ref = refs
    objects = packed_ref.shape[1]
    last = packed_ref.shape[0] - 1
    one = jnp.ones((GROUP, objects), jnp.float32)
    zero = jnp.zeros((GROUP, objects), jnp.float32)
    depth = GROUP * KINDS
    basis = basis_ref[...]
    blank = jnp.zeros((depth, objects), jnp.bfloat16)
    scale_ref[...] = 1.0 / (spread_ref[...] + packed_ref[last:])
    lane = lax.broadcasted_iota(jnp.int32, (objects, 2 * depth), 1) % GROUP
    total = jnp.zeros((objects, objects), jnp.float32)
    blocks = []
    for window in range(last // (AXES * basis.shape[1] // 6)):
        for high, low, length in features(position_rows(basis, packed_ref, window)):
            stack = jnp.concatenate(high + low + high + [one, one, one] + length + [zero], axis=0)
            blocks.append(stack.astype(jnp.bfloat16))
    for pair in range(len(blocks) // 2):
        left = jnp.concatenate([left_ref[2 * pair], left_ref[2 * pair + 1]], axis=1)
        right = jnp.concatenate([
            jnp.concatenate([blocks[2 * pair], blank], axis=1),
            jnp.concatenate([blank, blocks[2 * pair + 1]], axis=1),
        ], axis=0)
        for sample in range(GROUP):
            chosen = jnp.where(lane == sample, left, jnp.zeros_like(left))
            squared = jnp.dot(chosen, right, preferred_element_type=jnp.float32)
            scale = scale_ref[...]
            total = total + (jnp.exp2(squared[:, :objects] * scale) + jnp.exp2(squared[:, objects:] * scale))
    rows = lax.dot_general(
        jnp.ones((8, objects), jnp.float32), total, (((1,), (1,)), ((), ())),
        precision=lax.Precision.HIGHEST, preferred_element_type=jnp.float32,
    )
    out_ref[...] = earlier[0][...] if earlier else jnp.zeros_like(out_ref)
    out_ref[place:place + 1] = rows[:1]


def own_side(basis, packed, mask, windows, partner_count, places_of, factor):
    objects = packed.shape[1]
    return pl.pallas_call(
        functools.partial(own_kernel, places_of, factor),
        out_shape=(
            jax.ShapeDtypeStruct((windows * SAMP // GROUP, objects, GROUP * KINDS), jnp.bfloat16),
            jax.ShapeDtypeStruct((objects, objects), jnp.float32),
            jax.ShapeDtypeStruct((partner_count, ROUNDS, objects), jnp.float32),
        ),
        in_specs=[VMEM] * 3,
        out_specs=(VMEM,) * 3,
        name="own_side",
        compiler_params=pltpu.CompilerParams(vmem_limit_bytes=16 << 20),
        cost_estimate=pl.CostEstimate(flops=10_000_000, bytes_accessed=1_000_000, transcendentals=0),
    )(basis, packed, mask)


def pair_side(place, basis, left, spread, packed, windows, earlier, partner_count):
    objects = packed.shape[1]
    pairs = windows * SAMP // GROUP // 2
    depth = 2 * GROUP * KINDS
    operands = (basis, left, spread, packed) + (() if earlier is None else (earlier,))
    return pl.pallas_call(
        functools.partial(pair_kernel, place),
        out_shape=jax.ShapeDtypeStruct((partner_count, objects), jnp.float32),
        in_specs=[VMEM] * len(operands),
        out_specs=VMEM,
        scratch_shapes=[pltpu.VMEM((objects, objects), jnp.float32)],
        name="pair_side",
        compiler_params=pltpu.CompilerParams(vmem_limit_bytes=16 << 20),
        cost_estimate=pl.CostEstimate(
            flops=2 * pairs * GROUP * objects * depth * 2 * objects,
            bytes_accessed=4_000_000,
            transcendentals=windows * SAMP * objects * objects,
        ),
    )(*operands)


def direct_plan(plane_count):
    steps, places = [], []
    for round_no in range(ROUNDS):
        step = (round_no // 2 + 1) * (1 if round_no % 2 == 0 else -1) % plane_count
        if step not in steps:
            steps.append(step)
        places.append(steps.index(step))
    return [[(g, (g + step) % plane_count) for g in range(plane_count)] for step in steps], places


def rotated_places():
    odd = lax.axis_index("plane") % 2
    return [1 - odd, odd, 2, 2]


def hops(times):
    bits = times.bit_length() - 1
    rounds = [[lambda time, bit=bit: time ^ (1 << bit)] for bit in reversed(range(bits))]
    if bits % 2:
        ring = (0, 1, 3, 2)

        def turned(time, turn):
            return time & ~3 | ring[(ring.index(time & 3) + turn) % 4]

        rounds[-2:] = [[lambda time, turn=turn: turned(time, turn) for turn in (1, 3, 2)]]
    return rounds


def summed(value):
    planes, times = lax.axis_size("plane"), lax.axis_size("tm")
    if times & (times - 1) or times in (1, 2) or planes % 2:
        return lax.psum(value, "tm")

    def moved(array, hop):
        pairs = [
            (plane * times + time, (plane ^ 1) * times + hop(time))
            for plane in range(planes) for time in range(times)
        ]
        return lax.ppermute(array, ("plane", "tm"), pairs)

    for steps in hops(times):
        parts = [moved(value, hop) for hop in steps + [lambda time: time]]
        value = sum(parts[1:], parts[0])
    return value


def local(coeffs, radius, tile_mask):
    windows, _, degrees, objects = coeffs.shape
    planes, times = lax.axis_size("plane"), lax.axis_size("tm")
    packed, mask, basis = stage(coeffs, radius, tile_mask, jnp.asarray(basis_parts(degrees)))
    factor = 1.0 / (windows * times * SAMP * objects)

    if planes == 4:
        near = lax.ppermute(packed, "plane", [(g, g ^ 1) for g in range(4)])
        across = lax.ppermute(packed, "plane", [(g, g ^ 3) for g in range(4)])
        left, spread, weight = own_side(basis, packed, mask, windows, 3, rotated_places, factor)
        sums = pair_side(0, basis, left, spread, near, windows, None, 3)
        across, sums = lax.optimization_barrier((across, sums))
        relayed = lax.ppermute(across, "plane", [(g, g ^ 1) for g in range(4)])
        sums = pair_side(1, basis, left, spread, across, windows, sums, 3)
        sums = pair_side(2, basis, left, spread, relayed, windows, sums, 3)
    else:
        moves, places = direct_plan(planes)
        others = [lax.ppermute(packed, "plane", move) for move in moves]
        left, spread, weight = own_side(basis, packed, mask, windows, len(moves), lambda: places, factor)
        sums = None
        for place, other in enumerate(others):
            sums = pair_side(place, basis, left, spread, other, windows, sums, len(moves))
    sums = summed(sums)
    return sum(weight[place] * sums[place:place + 1] for place in range(weight.shape[0]))


def solution(mesh):
    placed = (P("tm", None, None, "plane"), P("plane"), P(None, "plane", None))
    return jax.shard_map(
        local, mesh=mesh, in_specs=placed, out_specs=P(None, "plane"), check_vma=False
    )
```

```python
import functools
import math

import jax
import jax.numpy as jnp
from jax import lax
from jax.experimental import pallas as pl
from jax.experimental.pallas import tpu as pltpu
from jax.sharding import PartitionSpec as P


SAMP = 32
ROUNDS = 4
AXES = 3
GROUP = 8
KINDS = 16
VMEM = pl.BlockSpec(memory_space=pltpu.VMEM)


def thirds(value):
    first = value.astype(jnp.bfloat16).astype(jnp.float32)
    rest = value - first
    second = rest.astype(jnp.bfloat16).astype(jnp.float32)
    third = (rest - second).astype(jnp.bfloat16).astype(jnp.float32)
    return first, second, third


def basis_parts(degrees):
    shape = (SAMP, 6 * degrees)
    sample = lax.broadcasted_iota(jnp.int32, shape, 0).astype(jnp.float32)
    lane = lax.broadcasted_iota(jnp.int32, shape, 1)
    nodes = -1.0 + (2.0 * sample + 1.0) / SAMP
    degree_of = lane % degrees
    before, current = jnp.ones(shape, jnp.float32), nodes
    basis = jnp.where(degree_of == 0, before, current)
    for degree in range(2, degrees):
        before, current = current, 2.0 * nodes * current - before
        basis = jnp.where(degree_of == degree, current, basis)
    first, second, third = thirds(basis * math.sqrt(1.0 / math.log(2.0)))
    part = lane // degrees
    late = jnp.where(part == 5, third, second)
    return jnp.where((part < 2) | (part == 4), first, late).astype(jnp.bfloat16)


def position_rows(basis, coeffs_ref, window):
    columns = []
    for axis in range(AXES):
        a, b, c = (part.astype(jnp.bfloat16) for part in thirds(coeffs_ref[window, axis]))
        columns.append(jnp.concatenate([a, b, a, b, c, a], axis=0))
    stacked = jnp.concatenate(columns, axis=1)
    rows = jnp.dot(basis, stacked, preferred_element_type=jnp.float32)
    width = coeffs_ref.shape[3]
    return [rows[:, axis * width:(axis + 1) * width] for axis in range(AXES)]


def features(rows):
    found = []
    for start in range(0, SAMP, GROUP):
        high, low, length = [], [], None
        for row in rows:
            value = row[start:start + GROUP]
            top = value.astype(jnp.bfloat16).astype(jnp.float32)
            bottom = (value - top).astype(jnp.bfloat16).astype(jnp.float32)
            kept = top + bottom
            length = kept * kept if length is None else length + kept * kept
            high.append(top)
            low.append(bottom)
        found.append((high, low, list(thirds(-length))))
    return found


def facing_blocks(basis, coeffs_ref):
    one = jnp.ones((GROUP, coeffs_ref.shape[3]), jnp.float32)
    blocks = []
    for window in range(coeffs_ref.shape[0]):
        for high, low, length in features(position_rows(basis, coeffs_ref, window)):
            stack = jnp.concatenate(high + low + high + [one, one, one] + length + [0.0 * one], axis=0)
            blocks.append(stack.astype(jnp.bfloat16))
    return blocks


def own_blocks(basis, coeffs_ref, left_ref):
    one = jnp.ones((GROUP, coeffs_ref.shape[3]), jnp.float32)
    place = 0
    for window in range(coeffs_ref.shape[0]):
        for high, low, length in features(position_rows(basis, coeffs_ref, window)):
            high = [2.0 * value for value in high]
            low = [2.0 * value for value in low]
            stack = jnp.concatenate(high + high + low + length + [one, one, one, 0.0 * one], axis=0)
            left_ref[place] = stack.T.astype(jnp.bfloat16)
            place += 1


def hazard_row(left_ref, blocks, scale_ref):
    objects = scale_ref.shape[0]
    depth = GROUP * KINDS
    blank = jnp.zeros((depth, objects), jnp.bfloat16)
    lane = lax.broadcasted_iota(jnp.int32, (objects, 2 * depth), 1) % GROUP
    total = jnp.zeros((objects, objects), jnp.float32)
    for pair in range(len(blocks) // 2):
        left = jnp.concatenate([left_ref[2 * pair], left_ref[2 * pair + 1]], axis=1)
        right = jnp.concatenate([
            jnp.concatenate([blocks[2 * pair], blank], axis=1),
            jnp.concatenate([blank, blocks[2 * pair + 1]], axis=1),
        ], axis=0)
        for sample in range(GROUP):
            chosen = jnp.where(lane == sample, left, jnp.zeros_like(left))
            squared = jnp.dot(chosen, right, preferred_element_type=jnp.float32)
            scale = scale_ref[...]
            total = total + (jnp.exp2(squared[:, :objects] * scale) + jnp.exp2(squared[:, objects:] * scale))
    return lax.dot_general(
        jnp.ones((8, objects), jnp.float32), total, (((1,), (1,)), ((), ())),
        precision=lax.Precision.HIGHEST, preferred_element_type=jnp.float32,
    )


def own_kernel(
    places_of, factor, coeffs_hbm, mask_hbm, radius_ref,
    weight_ref, left_ref, spread_ref, basis_ref, coeffs_ref, mask_ref, sems,
):
    copies = [
        pltpu.make_async_copy(coeffs_hbm, coeffs_ref, sems.at[0]),
        pltpu.make_async_copy(mask_hbm, mask_ref, sems.at[1]),
    ]
    for copy in copies:
        copy.start()
    objects = coeffs_ref.shape[3]
    basis = basis_parts(coeffs_ref.shape[2])
    basis_ref[...] = basis
    spread_ref[...] = jnp.broadcast_to(radius_ref[...], spread_ref.shape).T
    for copy in copies:
        copy.wait()
    own_blocks(basis, coeffs_ref, left_ref)
    weight_ref[...] = jnp.zeros_like(weight_ref)
    for round_no, chosen in enumerate(places_of()):
        screened = jnp.broadcast_to(mask_ref[:, round_no:round_no + 1], (1, objects)).astype(jnp.float32) * factor
        for index in range(weight_ref.shape[0]):
            weight_ref[index, round_no:round_no + 1] = jnp.where(chosen == index, screened, 0.0)


def pair_kernel(place, basis_ref, left_ref, spread_ref, coeffs_ref, radius_ref, *refs):
    *earlier, sums_ref, scale_ref = refs
    blocks = facing_blocks(basis_ref[...], coeffs_ref)
    scale_ref[...] = 1.0 / (spread_ref[...] + radius_ref[...])
    row = hazard_row(left_ref, blocks, scale_ref)
    sums_ref[...] = earlier[0][...] if earlier else jnp.zeros_like(sums_ref)
    sums_ref[place:place + 1] = row[:1]


def own_side(coeffs, mask, radius, partner_count, places_of, factor):
    windows, _, degrees, objects = coeffs.shape
    weight, left, spread, basis = pl.pallas_call(
        functools.partial(own_kernel, places_of, factor),
        out_shape=(
            jax.ShapeDtypeStruct((partner_count, ROUNDS, objects), jnp.float32),
            jax.ShapeDtypeStruct((windows * SAMP // GROUP, objects, GROUP * KINDS), jnp.bfloat16),
            jax.ShapeDtypeStruct((objects, objects), jnp.float32),
            jax.ShapeDtypeStruct((SAMP, 6 * degrees), jnp.bfloat16),
        ),
        in_specs=[pl.BlockSpec(memory_space=pltpu.HBM)] * 2 + [VMEM],
        out_specs=(VMEM,) * 4,
        scratch_shapes=[
            pltpu.VMEM(coeffs.shape, coeffs.dtype),
            pltpu.VMEM(mask.shape, mask.dtype),
            pltpu.SemaphoreType.DMA((2,)),
        ],
        name="own_side",
        compiler_params=pltpu.CompilerParams(vmem_limit_bytes=16 << 20),
        cost_estimate=pl.CostEstimate(flops=10_000_000, bytes_accessed=1_000_000, transcendentals=0),
    )(
        pltpu.with_memory_space_constraint(coeffs, pltpu.HBM),
        pltpu.with_memory_space_constraint(mask, pltpu.HBM),
        radius,
    )
    return weight, (basis, left, spread)


def pair_side(place, given, coeffs, radius, sums, partner_count):
    windows, _, _, objects = coeffs.shape
    operands = (*given, coeffs, radius) + (() if sums is None else (sums,))
    return pl.pallas_call(
        functools.partial(pair_kernel, place),
        out_shape=jax.ShapeDtypeStruct((partner_count, objects), jnp.float32),
        in_specs=[VMEM] * len(operands),
        out_specs=VMEM,
        scratch_shapes=[pltpu.VMEM((objects, objects), jnp.float32)],
        name="pair_side",
        compiler_params=pltpu.CompilerParams(vmem_limit_bytes=16 << 20),
        cost_estimate=pl.CostEstimate(
            flops=windows * SAMP * 4 * GROUP * KINDS * objects * objects,
            bytes_accessed=4_000_000,
            transcendentals=windows * SAMP * objects * objects,
        ),
    )(*operands)


def direct_plan(plane_count):
    steps, places = [], []
    for round_no in range(ROUNDS):
        step = (round_no // 2 + 1) * (1 if round_no % 2 == 0 else -1) % plane_count
        if step not in steps:
            steps.append(step)
        places.append(steps.index(step))
    return [[(g, (g + step) % plane_count) for g in range(plane_count)] for step in steps], places


def rotated_places():
    odd = lax.axis_index("plane") % 2
    return [1 - odd, odd, 2, 2]


def hops(times):
    bits = times.bit_length() - 1
    rounds = [[lambda time, bit=bit: time ^ (1 << bit)] for bit in reversed(range(bits))]
    if bits % 2:
        ring = (0, 1, 3, 2)

        def turned(time, turn):
            return time & ~3 | ring[(ring.index(time & 3) + turn) % 4]

        rounds[-2:] = [[lambda time, turn=turn: turned(time, turn) for turn in (1, 3, 2)]]
    return rounds


def summed(value):
    planes, times = lax.axis_size("plane"), lax.axis_size("tm")
    if times & (times - 1) or times in (1, 2) or planes % 2:
        return lax.psum(value, "tm")

    def moved(array, hop):
        pairs = [
            (plane * times + time, (plane ^ 1) * times + hop(time))
            for plane in range(planes) for time in range(times)
        ]
        return lax.ppermute(array, ("plane", "tm"), pairs)

    for steps in hops(times):
        parts = [moved(value, hop) for hop in steps + [lambda time: time]]
        value = sum(parts[1:], parts[0])
    return value


def local(coeffs, radius, tile_mask):
    windows, _, _, objects = coeffs.shape
    planes, times = lax.axis_size("plane"), lax.axis_size("tm")
    mask = tile_mask.reshape(1, ROUNDS)
    row = radius[None, :]
    factor = 1.0 / (windows * times * SAMP * objects)

    def taken(value, move):
        return lax.ppermute(value, "plane", move)

    def own(partner_count, places_of):
        return own_side(coeffs, mask, row, partner_count, places_of, factor)

    if planes == 4:
        beside = [(g, g ^ 1) for g in range(4)]
        opposite = [(g, g ^ 3) for g in range(4)]
        near = taken(coeffs, beside)
        across = taken(coeffs, opposite)
        near_row = taken(row, beside)
        across_row = taken(row, opposite)
        weight, given = own(3, rotated_places)
        sums = pair_side(0, given, near, near_row, None, 3)
        across, across_row, sums = lax.optimization_barrier((across, across_row, sums))
        relayed = taken(across, beside)
        relayed_row = taken(across_row, beside)
        sums = pair_side(1, given, across, across_row, sums, 3)
        sums = pair_side(2, given, relayed, relayed_row, sums, 3)
    else:
        moves, places = direct_plan(planes)
        others = [(lax.ppermute(coeffs, "plane", move), lax.ppermute(row, "plane", move)) for move in moves]
        weight, given = own(len(moves), lambda: places)
        sums = None
        for place, other in enumerate(others):
            sums = pair_side(place, given, *other, sums, len(moves))
    sums = summed(sums)
    return sum(weight[place] * sums[place:place + 1] for place in range(weight.shape[0]))


def solution(mesh):
    placed = (P("tm", None, None, "plane"), P("plane"), P(None, "plane", None))
    return jax.shard_map(
        local, mesh=mesh, in_specs=placed, out_specs=P(None, "plane"), check_vma=False
    )
```

```python
import functools
import math

import jax
import jax.numpy as jnp
from jax import lax
from jax.experimental import pallas as pl
from jax.experimental.pallas import tpu as pltpu
from jax.sharding import PartitionSpec as P


SAMP = 32
ROUNDS = 4
AXES = 3
GROUP = 8
KINDS = 16
VMEM = pl.BlockSpec(memory_space=pltpu.VMEM)


def thirds(value):
    first = value.astype(jnp.bfloat16).astype(jnp.float32)
    rest = value - first
    second = rest.astype(jnp.bfloat16).astype(jnp.float32)
    third = (rest - second).astype(jnp.bfloat16).astype(jnp.float32)
    return first, second, third


def basis_parts(degrees):
    shape = (SAMP, 6 * degrees)
    sample = lax.broadcasted_iota(jnp.int32, shape, 0).astype(jnp.float32)
    lane = lax.broadcasted_iota(jnp.int32, shape, 1)
    nodes = -1.0 + (2.0 * sample + 1.0) / SAMP
    degree_of = lane % degrees
    before, current = jnp.ones(shape, jnp.float32), nodes
    basis = jnp.where(degree_of == 0, before, current)
    for degree in range(2, degrees):
        before, current = current, 2.0 * nodes * current - before
        basis = jnp.where(degree_of == degree, current, basis)
    first, second, third = thirds(basis * math.sqrt(1.0 / math.log(2.0)))
    part = lane // degrees
    late = jnp.where(part == 5, third, second)
    return jnp.where((part < 2) | (part == 4), first, late).astype(jnp.bfloat16)


def position_rows(basis, coeffs_ref, window):
    columns = []
    for axis in range(AXES):
        a, b, c = (part.astype(jnp.bfloat16) for part in thirds(coeffs_ref[window, axis]))
        columns.append(jnp.concatenate([a, b, a, b, c, a], axis=0))
    stacked = jnp.concatenate(columns, axis=1)
    rows = jnp.dot(basis, stacked, preferred_element_type=jnp.float32)
    width = coeffs_ref.shape[3]
    return [rows[:, axis * width:(axis + 1) * width] for axis in range(AXES)]


def features(rows):
    found = []
    for start in range(0, SAMP, GROUP):
        high, low, length = [], [], None
        for row in rows:
            value = row[start:start + GROUP]
            top = value.astype(jnp.bfloat16).astype(jnp.float32)
            bottom = (value - top).astype(jnp.bfloat16).astype(jnp.float32)
            kept = top + bottom
            length = kept * kept if length is None else length + kept * kept
            high.append(top)
            low.append(bottom)
        found.append((high, low, list(thirds(-length))))
    return found


def facing_blocks(basis, coeffs_ref):
    one = jnp.ones((GROUP, coeffs_ref.shape[3]), jnp.float32)
    blocks = []
    for window in range(coeffs_ref.shape[0]):
        for high, low, length in features(position_rows(basis, coeffs_ref, window)):
            stack = jnp.concatenate(high + low + high + [one, one, one] + length + [0.0 * one], axis=0)
            blocks.append(stack.astype(jnp.bfloat16))
    return blocks


def own_blocks(basis, coeffs_ref, left_ref):
    one = jnp.ones((GROUP, coeffs_ref.shape[3]), jnp.float32)
    place = 0
    for window in range(coeffs_ref.shape[0]):
        for high, low, length in features(position_rows(basis, coeffs_ref, window)):
            high = [2.0 * value for value in high]
            low = [2.0 * value for value in low]
            stack = jnp.concatenate(high + high + low + length + [one, one, one, 0.0 * one], axis=0)
            left_ref[place] = stack.T.astype(jnp.bfloat16)
            place += 1


def hazard_row(left_ref, blocks, scale_ref):
    objects = scale_ref.shape[0]
    depth = GROUP * KINDS
    blank = jnp.zeros((depth, objects), jnp.bfloat16)
    lane = lax.broadcasted_iota(jnp.int32, (objects, 2 * depth), 1) % GROUP
    total = jnp.zeros((objects, objects), jnp.float32)
    for pair in range(len(blocks) // 2):
        left = jnp.concatenate([left_ref[2 * pair], left_ref[2 * pair + 1]], axis=1)
        right = jnp.concatenate([
            jnp.concatenate([blocks[2 * pair], blank], axis=1),
            jnp.concatenate([blank, blocks[2 * pair + 1]], axis=1),
        ], axis=0)
        for sample in range(GROUP):
            chosen = jnp.where(lane == sample, left, jnp.zeros_like(left))
            squared = jnp.dot(chosen, right, preferred_element_type=jnp.float32)
            scale = scale_ref[...]
            total = total + (jnp.exp2(squared[:, :objects] * scale) + jnp.exp2(squared[:, objects:] * scale))
    return lax.dot_general(
        jnp.ones((8, objects), jnp.float32), total, (((1,), (1,)), ((), ())),
        precision=lax.Precision.HIGHEST, preferred_element_type=jnp.float32,
    )


def own_kernel(
    places_of, factor, coeffs_hbm, mask_hbm, radius_ref, near_ref,
    weight_ref, left_ref, spread_ref, basis_ref, blocks_ref, coeffs_ref, mask_ref, sems,
):
    copies = [
        pltpu.make_async_copy(coeffs_hbm, coeffs_ref, sems.at[0]),
        pltpu.make_async_copy(mask_hbm, mask_ref, sems.at[1]),
    ]
    for copy in copies:
        copy.start()
    objects = coeffs_ref.shape[3]
    basis = basis_parts(coeffs_ref.shape[2])
    basis_ref[...] = basis
    spread_ref[...] = jnp.broadcast_to(radius_ref[...], spread_ref.shape).T
    for place, block in enumerate(facing_blocks(basis, near_ref)):
        blocks_ref[place] = block
    for copy in copies:
        copy.wait()
    own_blocks(basis, coeffs_ref, left_ref)
    weight_ref[...] = jnp.zeros_like(weight_ref)
    for round_no, chosen in enumerate(places_of()):
        screened = jnp.broadcast_to(mask_ref[:, round_no:round_no + 1], (1, objects)).astype(jnp.float32) * factor
        for index in range(weight_ref.shape[0]):
            weight_ref[index, round_no:round_no + 1] = jnp.where(chosen == index, screened, 0.0)


def pair_kernel(place, basis_ref, left_ref, spread_ref, coeffs_ref, radius_ref, *refs):
    *earlier, sums_ref, scale_ref = refs
    if place == 0:
        blocks = [coeffs_ref[group] for group in range(coeffs_ref.shape[0])]
    else:
        blocks = facing_blocks(basis_ref[...], coeffs_ref)
    scale_ref[...] = 1.0 / (spread_ref[...] + radius_ref[...])
    row = hazard_row(left_ref, blocks, scale_ref)
    sums_ref[...] = earlier[0][...] if earlier else jnp.zeros_like(sums_ref)
    sums_ref[place:place + 1] = row[:1]


def own_side(coeffs, mask, radius, near, partner_count, places_of, factor):
    windows, _, degrees, objects = coeffs.shape
    weight, left, spread, basis, blocks = pl.pallas_call(
        functools.partial(own_kernel, places_of, factor),
        out_shape=(
            jax.ShapeDtypeStruct((partner_count, ROUNDS, objects), jnp.float32),
            jax.ShapeDtypeStruct((windows * SAMP // GROUP, objects, GROUP * KINDS), jnp.bfloat16),
            jax.ShapeDtypeStruct((objects, objects), jnp.float32),
            jax.ShapeDtypeStruct((SAMP, 6 * degrees), jnp.bfloat16),
            jax.ShapeDtypeStruct((windows * SAMP // GROUP, GROUP * KINDS, objects), jnp.bfloat16),
        ),
        in_specs=[pl.BlockSpec(memory_space=pltpu.HBM)] * 2 + [VMEM] * 2,
        out_specs=(VMEM,) * 5,
        scratch_shapes=[
            pltpu.VMEM(coeffs.shape, coeffs.dtype),
            pltpu.VMEM(mask.shape, mask.dtype),
            pltpu.SemaphoreType.DMA((2,)),
        ],
        name="own_side",
        compiler_params=pltpu.CompilerParams(vmem_limit_bytes=16 << 20),
        cost_estimate=pl.CostEstimate(flops=10_000_000, bytes_accessed=1_000_000, transcendentals=0),
    )(
        pltpu.with_memory_space_constraint(coeffs, pltpu.HBM),
        pltpu.with_memory_space_constraint(mask, pltpu.HBM),
        radius, near,
    )
    return weight, (basis, left, spread), blocks


def pair_side(place, given, coeffs, radius, sums, partner_count):
    groups, objects, _ = given[1].shape
    windows = groups * GROUP // SAMP
    operands = (*given, coeffs, radius) + (() if sums is None else (sums,))
    return pl.pallas_call(
        functools.partial(pair_kernel, place),
        out_shape=jax.ShapeDtypeStruct((partner_count, objects), jnp.float32),
        in_specs=[VMEM] * len(operands),
        out_specs=VMEM,
        scratch_shapes=[pltpu.VMEM((objects, objects), jnp.float32)],
        name="pair_side",
        compiler_params=pltpu.CompilerParams(vmem_limit_bytes=16 << 20),
        cost_estimate=pl.CostEstimate(
            flops=windows * SAMP * 4 * GROUP * KINDS * objects * objects,
            bytes_accessed=4_000_000,
            transcendentals=windows * SAMP * objects * objects,
        ),
    )(*operands)


def direct_plan(plane_count):
    steps, places = [], []
    for round_no in range(ROUNDS):
        step = (round_no // 2 + 1) * (1 if round_no % 2 == 0 else -1) % plane_count
        if step not in steps:
            steps.append(step)
        places.append(steps.index(step))
    return [[(g, (g + step) % plane_count) for g in range(plane_count)] for step in steps], places


def rotated_places():
    odd = lax.axis_index("plane") % 2
    return [1 - odd, odd, 2, 2]


def hops(times):
    bits = times.bit_length() - 1
    rounds = [[lambda time, bit=bit: time ^ (1 << bit)] for bit in reversed(range(bits))]
    if bits % 2:
        ring = (0, 1, 3, 2)

        def turned(time, turn):
            return time & ~3 | ring[(ring.index(time & 3) + turn) % 4]

        rounds[-2:] = [[lambda time, turn=turn: turned(time, turn) for turn in (1, 3, 2)]]
    return rounds


def summed(value):
    planes, times = lax.axis_size("plane"), lax.axis_size("tm")
    if times & (times - 1) or times in (1, 2) or planes % 2:
        return lax.psum(value, "tm")

    def moved(array, hop):
        pairs = [
            (plane * times + time, (plane ^ 1) * times + hop(time))
            for plane in range(planes) for time in range(times)
        ]
        return lax.ppermute(array, ("plane", "tm"), pairs)

    for steps in hops(times):
        parts = [moved(value, hop) for hop in steps + [lambda time: time]]
        while len(parts) > 1:
            parts = [left + right for left, right in zip(parts[::2], parts[1::2])]
        value = parts[0]
    return value


def local(coeffs, radius, tile_mask):
    windows, _, _, objects = coeffs.shape
    planes, times = lax.axis_size("plane"), lax.axis_size("tm")
    mask = tile_mask.reshape(1, ROUNDS)
    row = radius[None, :]
    factor = 1.0 / (windows * times * SAMP * objects)

    def taken(value, move):
        return lax.ppermute(value, "plane", move)

    def own(near, partner_count, places_of):
        return own_side(coeffs, mask, row, near, partner_count, places_of, factor)

    if planes == 4:
        beside = [(g, g ^ 1) for g in range(4)]
        opposite = [(g, g ^ 3) for g in range(4)]
        near = taken(coeffs, beside)
        across = taken(coeffs, opposite)
        near_row = taken(row, beside)
        across_row = taken(row, opposite)
        weight, given, blocks = own(near, 3, rotated_places)
        sums = pair_side(0, given, blocks, near_row, None, 3)
        across, across_row, sums = lax.optimization_barrier((across, across_row, sums))
        relayed = taken(across, beside)
        relayed_row = taken(across_row, beside)
        sums = pair_side(1, given, across, across_row, sums, 3)
        sums = pair_side(2, given, relayed, relayed_row, sums, 3)
    else:
        moves, places = direct_plan(planes)
        others = [(lax.ppermute(coeffs, "plane", move), lax.ppermute(row, "plane", move)) for move in moves]
        weight, given, blocks = own(others[0][0], len(moves), lambda: places)
        sums = pair_side(0, given, blocks, others[0][1], None, len(moves))
        for place, other in enumerate(others[1:], 1):
            sums = pair_side(place, given, *other, sums, len(moves))
    sums = summed(sums)
    return sum(weight[place] * sums[place:place + 1] for place in range(weight.shape[0]))


def solution(mesh):
    placed = (P("tm", None, None, "plane"), P("plane"), P(None, "plane", None))
    return jax.shard_map(
        local, mesh=mesh, in_specs=placed, out_specs=P(None, "plane"), check_vma=False
    )
```

```python
import functools
import math

import jax
import jax.numpy as jnp
from jax import lax
from jax.experimental import pallas as pl
from jax.experimental.pallas import tpu as pltpu
from jax.sharding import PartitionSpec as P


SAMP = 32
ROUNDS = 4
AXES = 3
GROUP = 8
KINDS = 16
VMEM = pl.BlockSpec(memory_space=pltpu.VMEM)


def thirds(value):
    first = value.astype(jnp.bfloat16).astype(jnp.float32)
    rest = value - first
    second = rest.astype(jnp.bfloat16).astype(jnp.float32)
    third = (rest - second).astype(jnp.bfloat16).astype(jnp.float32)
    return first, second, third


def basis_parts(degrees):
    shape = (SAMP, 6 * degrees)
    sample = lax.broadcasted_iota(jnp.int32, shape, 0).astype(jnp.float32)
    lane = lax.broadcasted_iota(jnp.int32, shape, 1)
    nodes = -1.0 + (2.0 * sample + 1.0) / SAMP
    degree_of = lane % degrees
    before, current = jnp.ones(shape, jnp.float32), nodes
    basis = jnp.where(degree_of == 0, before, current)
    for degree in range(2, degrees):
        before, current = current, 2.0 * nodes * current - before
        basis = jnp.where(degree_of == degree, current, basis)
    first, second, third = thirds(basis * math.sqrt(1.0 / math.log(2.0)))
    part = lane // degrees
    late = jnp.where(part == 5, third, second)
    return jnp.where((part < 2) | (part == 4), first, late).astype(jnp.bfloat16)


def position_rows(basis, coeffs_ref, window):
    columns = []
    for axis in range(AXES):
        a, b, c = (part.astype(jnp.bfloat16) for part in thirds(coeffs_ref[window, axis]))
        columns.append(jnp.concatenate([a, b, a, b, c, a], axis=0))
    stacked = jnp.concatenate(columns, axis=1)
    rows = jnp.dot(basis, stacked, preferred_element_type=jnp.float32)
    width = coeffs_ref.shape[3]
    return [rows[:, axis * width:(axis + 1) * width] for axis in range(AXES)]


def features(rows):
    found = []
    for start in range(0, SAMP, GROUP):
        high, low, length = [], [], None
        for row in rows:
            value = row[start:start + GROUP]
            top = value.astype(jnp.bfloat16).astype(jnp.float32)
            bottom = (value - top).astype(jnp.bfloat16).astype(jnp.float32)
            kept = top + bottom
            length = kept * kept if length is None else length + kept * kept
            high.append(top)
            low.append(bottom)
        found.append((high, low, list(thirds(-length))[:2]))
    return found


def facing_blocks(basis, coeffs_ref):
    one = jnp.ones((GROUP, coeffs_ref.shape[3]), jnp.float32)
    blocks = []
    for window in range(coeffs_ref.shape[0]):
        for high, low, length in features(position_rows(basis, coeffs_ref, window)):
            stack = jnp.concatenate(high + low + high + low + [one, one] + length, axis=0)
            blocks.append(stack.astype(jnp.bfloat16))
    return blocks


def own_blocks(basis, coeffs_ref, left_ref):
    one = jnp.ones((GROUP, coeffs_ref.shape[3]), jnp.float32)
    place = 0
    for window in range(coeffs_ref.shape[0]):
        for high, low, length in features(position_rows(basis, coeffs_ref, window)):
            high = [2.0 * value for value in high]
            low = [2.0 * value for value in low]
            stack = jnp.concatenate(high + high + low + low + length + [one, one], axis=0)
            left_ref[place] = stack.T.astype(jnp.bfloat16)
            place += 1


def hazard_row(left_ref, blocks, scale_ref):
    objects = scale_ref.shape[0]
    depth = GROUP * KINDS
    blank = jnp.zeros((depth, objects), jnp.bfloat16)
    lane = lax.broadcasted_iota(jnp.int32, (objects, 2 * depth), 1) % GROUP
    total = jnp.zeros((objects, objects), jnp.float32)
    for pair in range(len(blocks) // 2):
        left = jnp.concatenate([left_ref[2 * pair], left_ref[2 * pair + 1]], axis=1)
        right = jnp.concatenate([
            jnp.concatenate([blocks[2 * pair], blank], axis=1),
            jnp.concatenate([blank, blocks[2 * pair + 1]], axis=1),
        ], axis=0)
        for sample in range(GROUP):
            chosen = jnp.where(lane == sample, left, jnp.zeros_like(left))
            squared = jnp.dot(chosen, right, preferred_element_type=jnp.float32)
            scale = scale_ref[...]
            total = total + (jnp.exp2(squared[:, :objects] * scale) + jnp.exp2(squared[:, objects:] * scale))
    return lax.dot_general(
        jnp.ones((8, objects), jnp.float32), total, (((1,), (1,)), ((), ())),
        precision=lax.Precision.HIGHEST, preferred_element_type=jnp.float32,
    )


def own_kernel(
    places_of, factor, coeffs_hbm, mask_hbm, radius_ref, near_ref,
    weight_ref, left_ref, spread_ref, basis_ref, blocks_ref, coeffs_ref, mask_ref, sems,
):
    copies = [
        pltpu.make_async_copy(coeffs_hbm, coeffs_ref, sems.at[0]),
        pltpu.make_async_copy(mask_hbm, mask_ref, sems.at[1]),
    ]
    for copy in copies:
        copy.start()
    objects = coeffs_ref.shape[3]
    basis = basis_parts(coeffs_ref.shape[2])
    basis_ref[...] = basis
    spread_ref[...] = jnp.broadcast_to(radius_ref[...], spread_ref.shape).T
    for place, block in enumerate(facing_blocks(basis, near_ref)):
        blocks_ref[place] = block
    for copy in copies:
        copy.wait()
    own_blocks(basis, coeffs_ref, left_ref)
    weight_ref[...] = jnp.zeros_like(weight_ref)
    for round_no, chosen in enumerate(places_of()):
        screened = jnp.broadcast_to(mask_ref[:, round_no:round_no + 1], (1, objects)).astype(jnp.float32) * factor
        for index in range(weight_ref.shape[0]):
            weight_ref[index, round_no:round_no + 1] = jnp.where(chosen == index, screened, 0.0)


def pair_kernel(place, basis_ref, left_ref, spread_ref, coeffs_ref, radius_ref, *refs):
    *earlier, sums_ref, scale_ref = refs
    if place == 0:
        blocks = [coeffs_ref[group] for group in range(coeffs_ref.shape[0])]
    else:
        blocks = facing_blocks(basis_ref[...], coeffs_ref)
    scale_ref[...] = 1.0 / (spread_ref[...] + radius_ref[...])
    row = hazard_row(left_ref, blocks, scale_ref)
    sums_ref[...] = earlier[0][...] if earlier else jnp.zeros_like(sums_ref)
    sums_ref[place:place + 1] = row[:1]


def own_side(coeffs, mask, radius, near, partner_count, places_of, factor):
    windows, _, degrees, objects = coeffs.shape
    weight, left, spread, basis, blocks = pl.pallas_call(
        functools.partial(own_kernel, places_of, factor),
        out_shape=(
            jax.ShapeDtypeStruct((partner_count, ROUNDS, objects), jnp.float32),
            jax.ShapeDtypeStruct((windows * SAMP // GROUP, objects, GROUP * KINDS), jnp.bfloat16),
            jax.ShapeDtypeStruct((objects, objects), jnp.float32),
            jax.ShapeDtypeStruct((SAMP, 6 * degrees), jnp.bfloat16),
            jax.ShapeDtypeStruct((windows * SAMP // GROUP, GROUP * KINDS, objects), jnp.bfloat16),
        ),
        in_specs=[pl.BlockSpec(memory_space=pltpu.HBM)] * 2 + [VMEM] * 2,
        out_specs=(VMEM,) * 5,
        scratch_shapes=[
            pltpu.VMEM(coeffs.shape, coeffs.dtype),
            pltpu.VMEM(mask.shape, mask.dtype),
            pltpu.SemaphoreType.DMA((2,)),
        ],
        name="own_side",
        compiler_params=pltpu.CompilerParams(vmem_limit_bytes=16 << 20),
        cost_estimate=pl.CostEstimate(flops=10_000_000, bytes_accessed=1_000_000, transcendentals=0),
    )(
        pltpu.with_memory_space_constraint(coeffs, pltpu.HBM),
        pltpu.with_memory_space_constraint(mask, pltpu.HBM),
        radius, near,
    )
    return weight, (basis, left, spread), blocks


def pair_side(place, given, coeffs, radius, sums, partner_count):
    groups, objects, _ = given[1].shape
    windows = groups * GROUP // SAMP
    operands = (*given, coeffs, radius) + (() if sums is None else (sums,))
    return pl.pallas_call(
        functools.partial(pair_kernel, place),
        out_shape=jax.ShapeDtypeStruct((partner_count, objects), jnp.float32),
        in_specs=[VMEM] * len(operands),
        out_specs=VMEM,
        scratch_shapes=[pltpu.VMEM((objects, objects), jnp.float32)],
        name="pair_side",
        compiler_params=pltpu.CompilerParams(vmem_limit_bytes=16 << 20),
        cost_estimate=pl.CostEstimate(
            flops=windows * SAMP * 4 * GROUP * KINDS * objects * objects,
            bytes_accessed=4_000_000,
            transcendentals=windows * SAMP * objects * objects,
        ),
    )(*operands)


def direct_plan(plane_count):
    steps, places = [], []
    for round_no in range(ROUNDS):
        step = (round_no // 2 + 1) * (1 if round_no % 2 == 0 else -1) % plane_count
        if step not in steps:
            steps.append(step)
        places.append(steps.index(step))
    return [[(g, (g + step) % plane_count) for g in range(plane_count)] for step in steps], places


def rotated_places():
    odd = lax.axis_index("plane") % 2
    return [1 - odd, odd, 2, 2]


def hops(times):
    bits = times.bit_length() - 1
    rounds = [[lambda time, bit=bit: time ^ (1 << bit)] for bit in reversed(range(bits))]
    if bits % 2:
        ring = (0, 1, 3, 2)

        def turned(time, turn):
            return time & ~3 | ring[(ring.index(time & 3) + turn) % 4]

        rounds[-2:] = [[lambda time, turn=turn: turned(time, turn) for turn in (1, 3, 2)]]
    return rounds


def summed(value):
    planes, times = lax.axis_size("plane"), lax.axis_size("tm")
    if times & (times - 1) or times in (1, 2) or planes % 2:
        return lax.psum(value, "tm")

    def moved(array, hop):
        pairs = [
            (plane * times + time, (plane ^ 1) * times + hop(time))
            for plane in range(planes) for time in range(times)
        ]
        return lax.ppermute(array, ("plane", "tm"), pairs)

    for steps in hops(times):
        parts = [moved(value, hop) for hop in steps + [lambda time: time]]
        while len(parts) > 1:
            parts = [left + right for left, right in zip(parts[::2], parts[1::2])]
        value = parts[0]
    return value


def local(coeffs, radius, tile_mask):
    windows, _, _, objects = coeffs.shape
    planes, times = lax.axis_size("plane"), lax.axis_size("tm")
    mask = tile_mask.reshape(1, ROUNDS)
    row = radius[None, :]
    factor = 1.0 / (windows * times * SAMP * objects)

    def taken(value, move):
        return lax.ppermute(value, "plane", move)

    def own(near, partner_count, places_of):
        return own_side(coeffs, mask, row, near, partner_count, places_of, factor)

    if planes == 4:
        beside = [(g, g ^ 1) for g in range(4)]
        opposite = [(g, g ^ 3) for g in range(4)]
        near = taken(coeffs, beside)
        across = taken(coeffs, opposite)
        near_row = taken(row, beside)
        across_row = taken(row, opposite)
        weight, given, blocks = own(near, 3, rotated_places)
        sums = pair_side(0, given, blocks, near_row, None, 3)
        across, across_row, sums = lax.optimization_barrier((across, across_row, sums))
        relayed = taken(across, beside)
        relayed_row = taken(across_row, beside)
        sums = pair_side(1, given, across, across_row, sums, 3)
        sums = pair_side(2, given, relayed, relayed_row, sums, 3)
    else:
        moves, places = direct_plan(planes)
        others = [(lax.ppermute(coeffs, "plane", move), lax.ppermute(row, "plane", move)) for move in moves]
        weight, given, blocks = own(others[0][0], len(moves), lambda: places)
        sums = pair_side(0, given, blocks, others[0][1], None, len(moves))
        for place, other in enumerate(others[1:], 1):
            sums = pair_side(place, given, *other, sums, len(moves))
    sums = summed(sums)
    return sum(weight[place] * sums[place:place + 1] for place in range(weight.shape[0]))


def solution(mesh):
    placed = (P("tm", None, None, "plane"), P("plane"), P(None, "plane", None))
    return jax.shard_map(
        local, mesh=mesh, in_specs=placed, out_specs=P(None, "plane"), check_vma=False
    )
```

```python
import functools
import math

import jax
import jax.numpy as jnp
from jax import lax
from jax.experimental import pallas as pl
from jax.experimental.pallas import tpu as pltpu
from jax.sharding import PartitionSpec as P


SAMP = 32
ROUNDS = 4
AXES = 3
GROUP = 8
KINDS = 16
VMEM = pl.BlockSpec(memory_space=pltpu.VMEM)


def thirds(value):
    first = value.astype(jnp.bfloat16).astype(jnp.float32)
    rest = value - first
    second = rest.astype(jnp.bfloat16).astype(jnp.float32)
    third = (rest - second).astype(jnp.bfloat16).astype(jnp.float32)
    return first, second, third


def basis_parts(degrees):
    shape = (SAMP, 6 * degrees)
    sample = lax.broadcasted_iota(jnp.int32, shape, 0).astype(jnp.float32)
    lane = lax.broadcasted_iota(jnp.int32, shape, 1)
    nodes = -1.0 + (2.0 * sample + 1.0) / SAMP
    degree_of = lane % degrees
    before, current = jnp.ones(shape, jnp.float32), nodes
    basis = jnp.where(degree_of == 0, before, current)
    for degree in range(2, degrees):
        before, current = current, 2.0 * nodes * current - before
        basis = jnp.where(degree_of == degree, current, basis)
    first, second, third = thirds(basis * math.sqrt(1.0 / math.log(2.0)))
    part = lane // degrees
    late = jnp.where(part == 5, third, second)
    return jnp.where((part < 2) | (part == 4), first, late).astype(jnp.bfloat16)


def position_rows(basis, coeffs_ref, window):
    columns = []
    for axis in range(AXES):
        a, b, c = (part.astype(jnp.bfloat16) for part in thirds(coeffs_ref[window, axis]))
        columns.append(jnp.concatenate([a, b, a, b, c, a], axis=0))
    stacked = jnp.concatenate(columns, axis=1)
    rows = jnp.dot(basis, stacked, preferred_element_type=jnp.float32)
    width = coeffs_ref.shape[3]
    return [rows[:, axis * width:(axis + 1) * width] for axis in range(AXES)]


def features(rows):
    found = []
    for start in range(0, SAMP, GROUP):
        high, low, length = [], [], None
        for row in rows:
            value = row[start:start + GROUP]
            top = value.astype(jnp.bfloat16).astype(jnp.float32)
            bottom = (value - top).astype(jnp.bfloat16).astype(jnp.float32)
            kept = top + bottom
            length = kept * kept if length is None else length + kept * kept
            high.append(top)
            low.append(bottom)
        found.append((high, low, list(thirds(-length))[:2]))
    return found


def facing_blocks(basis, coeffs_ref):
    one = jnp.ones((GROUP, coeffs_ref.shape[3]), jnp.float32)
    blocks = []
    for window in range(coeffs_ref.shape[0]):
        for high, low, length in features(position_rows(basis, coeffs_ref, window)):
            stack = jnp.concatenate(high + low + high + low + [one, one] + length, axis=0)
            blocks.append(stack.astype(jnp.bfloat16))
    return blocks


def own_blocks(basis, coeffs_ref, left_ref):
    one = jnp.ones((GROUP, coeffs_ref.shape[3]), jnp.float32)
    place = 0
    for window in range(coeffs_ref.shape[0]):
        for high, low, length in features(position_rows(basis, coeffs_ref, window)):
            high = [2.0 * value for value in high]
            low = [2.0 * value for value in low]
            stack = jnp.concatenate(high + high + low + low + length + [one, one], axis=0)
            left_ref[place] = stack.T.astype(jnp.bfloat16)
            place += 1


def hazard_row(left_ref, blocks, scale_ref):
    objects = scale_ref.shape[0]
    depth = GROUP * KINDS
    blank = jnp.zeros((depth, objects), jnp.bfloat16)
    lane = lax.broadcasted_iota(jnp.int32, (objects, 2 * depth), 1) % GROUP
    total = jnp.zeros((objects, objects), jnp.float32)
    for pair in range(len(blocks) // 2):
        left = jnp.concatenate([left_ref[2 * pair], left_ref[2 * pair + 1]], axis=1)
        right = jnp.concatenate([
            jnp.concatenate([blocks[2 * pair], blank], axis=1),
            jnp.concatenate([blank, blocks[2 * pair + 1]], axis=1),
        ], axis=0)
        for sample in range(GROUP):
            chosen = jnp.where(lane == sample, left, jnp.zeros_like(left))
            squared = jnp.dot(chosen, right, preferred_element_type=jnp.float32)
            scale = scale_ref[...]
            total = total + (jnp.exp2(squared[:, :objects] * scale) + jnp.exp2(squared[:, objects:] * scale))
    parts = jnp.concatenate([part.astype(jnp.bfloat16) for part in thirds(total)], axis=1)
    return lax.dot_general(
        jnp.ones((8, parts.shape[1]), jnp.bfloat16), parts, (((1,), (1,)), ((), ())),
        preferred_element_type=jnp.float32,
    )


def own_kernel(
    places_of, factor, coeffs_hbm, mask_hbm, radius_ref, near_ref,
    weight_ref, left_ref, spread_ref, basis_ref, blocks_ref, coeffs_ref, mask_ref, sems,
):
    copies = [
        pltpu.make_async_copy(coeffs_hbm, coeffs_ref, sems.at[0]),
        pltpu.make_async_copy(mask_hbm, mask_ref, sems.at[1]),
    ]
    for copy in copies:
        copy.start()
    objects = coeffs_ref.shape[3]
    basis = basis_parts(coeffs_ref.shape[2])
    basis_ref[...] = basis
    spread_ref[...] = jnp.broadcast_to(radius_ref[...], spread_ref.shape).T
    for place, block in enumerate(facing_blocks(basis, near_ref)):
        blocks_ref[place] = block
    for copy in copies:
        copy.wait()
    own_blocks(basis, coeffs_ref, left_ref)
    weight_ref[...] = jnp.zeros_like(weight_ref)
    for round_no, chosen in enumerate(places_of()):
        screened = jnp.broadcast_to(mask_ref[:, round_no:round_no + 1], (1, objects)).astype(jnp.float32) * factor
        for index in range(weight_ref.shape[0]):
            weight_ref[index, round_no:round_no + 1] = jnp.where(chosen == index, screened, 0.0)


def pair_kernel(place, basis_ref, left_ref, spread_ref, coeffs_ref, radius_ref, *refs):
    *earlier, sums_ref, scale_ref = refs
    if place == 0:
        blocks = [coeffs_ref[group] for group in range(coeffs_ref.shape[0])]
    else:
        blocks = facing_blocks(basis_ref[...], coeffs_ref)
    scale_ref[...] = 1.0 / (spread_ref[...] + radius_ref[...])
    row = hazard_row(left_ref, blocks, scale_ref)
    sums_ref[...] = earlier[0][...] if earlier else jnp.zeros_like(sums_ref)
    sums_ref[place:place + 1] = row[:1]


def own_side(coeffs, mask, radius, near, partner_count, places_of, factor):
    windows, _, degrees, objects = coeffs.shape
    weight, left, spread, basis, blocks = pl.pallas_call(
        functools.partial(own_kernel, places_of, factor),
        out_shape=(
            jax.ShapeDtypeStruct((partner_count, ROUNDS, objects), jnp.float32),
            jax.ShapeDtypeStruct((windows * SAMP // GROUP, objects, GROUP * KINDS), jnp.bfloat16),
            jax.ShapeDtypeStruct((objects, objects), jnp.float32),
            jax.ShapeDtypeStruct((SAMP, 6 * degrees), jnp.bfloat16),
            jax.ShapeDtypeStruct((windows * SAMP // GROUP, GROUP * KINDS, objects), jnp.bfloat16),
        ),
        in_specs=[pl.BlockSpec(memory_space=pltpu.HBM)] * 2 + [VMEM] * 2,
        out_specs=(VMEM,) * 5,
        scratch_shapes=[
            pltpu.VMEM(coeffs.shape, coeffs.dtype),
            pltpu.VMEM(mask.shape, mask.dtype),
            pltpu.SemaphoreType.DMA((2,)),
        ],
        name="own_side",
        compiler_params=pltpu.CompilerParams(vmem_limit_bytes=16 << 20),
        cost_estimate=pl.CostEstimate(flops=10_000_000, bytes_accessed=1_000_000, transcendentals=0),
    )(
        pltpu.with_memory_space_constraint(coeffs, pltpu.HBM),
        pltpu.with_memory_space_constraint(mask, pltpu.HBM),
        radius, near,
    )
    return weight, (basis, left, spread), blocks


def pair_side(place, given, coeffs, radius, sums, partner_count):
    groups, objects, _ = given[1].shape
    windows = groups * GROUP // SAMP
    operands = (*given, coeffs, radius) + (() if sums is None else (sums,))
    return pl.pallas_call(
        functools.partial(pair_kernel, place),
        out_shape=jax.ShapeDtypeStruct((partner_count, objects), jnp.float32),
        in_specs=[VMEM] * len(operands),
        out_specs=VMEM,
        scratch_shapes=[pltpu.VMEM((objects, objects), jnp.float32)],
        name="pair_side",
        compiler_params=pltpu.CompilerParams(vmem_limit_bytes=16 << 20),
        cost_estimate=pl.CostEstimate(
            flops=windows * SAMP * 4 * GROUP * KINDS * objects * objects,
            bytes_accessed=4_000_000,
            transcendentals=windows * SAMP * objects * objects,
        ),
    )(*operands)


def direct_plan(plane_count):
    steps, places = [], []
    for round_no in range(ROUNDS):
        step = (round_no // 2 + 1) * (1 if round_no % 2 == 0 else -1) % plane_count
        if step not in steps:
            steps.append(step)
        places.append(steps.index(step))
    return [[(g, (g + step) % plane_count) for g in range(plane_count)] for step in steps], places


def rotated_places():
    odd = lax.axis_index("plane") % 2
    return [1 - odd, odd, 2, 2]


def hops(times):
    bits = times.bit_length() - 1
    rounds = [[lambda time, bit=bit: time ^ (1 << bit)] for bit in reversed(range(bits))]
    if bits % 2:
        ring = (0, 1, 3, 2)

        def turned(time, turn):
            return time & ~3 | ring[(ring.index(time & 3) + turn) % 4]

        rounds[-2:] = [[lambda time, turn=turn: turned(time, turn) for turn in (1, 3, 2)]]
    return rounds


def summed(value):
    planes, times = lax.axis_size("plane"), lax.axis_size("tm")
    if times & (times - 1) or times in (1, 2) or planes % 2:
        return lax.psum(value, "tm")

    def moved(array, hop):
        pairs = [
            (plane * times + time, (plane ^ 1) * times + hop(time))
            for plane in range(planes) for time in range(times)
        ]
        return lax.ppermute(array, ("plane", "tm"), pairs)

    for steps in hops(times):
        parts = [moved(value, hop) for hop in steps + [lambda time: time]]
        while len(parts) > 1:
            parts = [left + right for left, right in zip(parts[::2], parts[1::2])]
        value = parts[0]
    return value


def local(coeffs, radius, tile_mask):
    windows, _, _, objects = coeffs.shape
    planes, times = lax.axis_size("plane"), lax.axis_size("tm")
    mask = tile_mask.reshape(1, ROUNDS)
    row = radius[None, :]
    factor = 1.0 / (windows * times * SAMP * objects)

    def taken(value, move):
        return lax.ppermute(value, "plane", move)

    def own(near, partner_count, places_of):
        return own_side(coeffs, mask, row, near, partner_count, places_of, factor)

    if planes == 4:
        beside = [(g, g ^ 1) for g in range(4)]
        opposite = [(g, g ^ 3) for g in range(4)]
        near = taken(coeffs, beside)
        across = taken(coeffs, opposite)
        near_row = taken(row, beside)
        across_row = taken(row, opposite)
        weight, given, blocks = own(near, 3, rotated_places)
        sums = pair_side(0, given, blocks, near_row, None, 3)
        across, across_row, sums = lax.optimization_barrier((across, across_row, sums))
        relayed = taken(across, beside)
        relayed_row = taken(across_row, beside)
        sums = pair_side(1, given, across, across_row, sums, 3)
        sums = pair_side(2, given, relayed, relayed_row, sums, 3)
    else:
        moves, places = direct_plan(planes)
        others = [(lax.ppermute(coeffs, "plane", move), lax.ppermute(row, "plane", move)) for move in moves]
        weight, given, blocks = own(others[0][0], len(moves), lambda: places)
        sums = pair_side(0, given, blocks, others[0][1], None, len(moves))
        for place, other in enumerate(others[1:], 1):
            sums = pair_side(place, given, *other, sums, len(moves))
    sums = summed(sums)
    return sum(weight[place] * sums[place:place + 1] for place in range(weight.shape[0]))


def solution(mesh):
    placed = (P("tm", None, None, "plane"), P("plane"), P(None, "plane", None))
    return jax.shard_map(
        local, mesh=mesh, in_specs=placed, out_specs=P(None, "plane"), check_vma=False
    )
```
